512 devices in a mesh: stn: 128 (over z, y, core), sec: 4 (over x).
Axes of the slice: x: 4, y: 8, z: 8, core: 2. Of those that a mesh axis runs over, the one named last changes fastest.
Arguments:
- voltages: bfloat16 [2, 128, 4, 2, 79872], P(None, 'stn', 'sec'), may hold values from -60 to 60
- bandpass: float32 [4, 6144], P('sec'), may hold values from 0.3 to 3
- station_flags: int32 [128], P('stn'), may hold values 0 or 1
- delays: int32 [256, 128], replicated, may hold values from 0 to 4095
- section: int32 [4], replicated, may hold values from 0 to 1, as said below
Outputs:
- visibilities: bfloat16 [4, 512, 256, 256], P('sec', 'stn')
- tied_beams: bfloat16 [4, 6144, 2, 2, 6, 256], P('sec', 'stn')
The draws below stay inside these ranges and needn't reach their ends.
Inputs may be any that keep to these rules, and one draw needn't show every extreme that they name: Exactly 1 coarse channels have section 1, the others 0.
All inputs are finite; a program needn't handle non-finite values. No bound on the sum of `station_flags` on one device may be relied on, other than what follows from the above.
Results may differ from the reference program's by a relative error of at most 0.0055.
Values may be sent and summed in bfloat16 or wider, within the bound.
A program may use at most 64 MiB of HBM per device.

```python
import math
import jax
import jax.numpy as jnp
from jax import lax

POLS = 2
NCH = 6144
TAPS = 8
FRAMES = 6
AVG = 12
BEAMS = 256
STATIONS = 128
COARSE = 4
VCH = 512


def draw_voltages(key, part):
    shape = (2, STATIONS, COARSE, POLS, (FRAMES + TAPS - 1) * NCH)
    key_base = jax.random.fold_in(key, 0)
    level = 1.0 + 2.0 * jnp.arange(COARSE).astype(jnp.float32) / (COARSE - 1)
    level = level[None, None, :, None, None]
    base = jnp.clip(jax.random.normal(key_base, shape, jnp.float32), -5.0, 5.0)
    return (base * level).astype(jnp.bfloat16)


def draw_section(key, part):
    order = jax.random.permutation(key, COARSE)
    return (order < COARSE // 4).astype(jnp.int32)


def place_ends(values, rng, smallest, high):
    dims = values.shape
    spot = [jax.random.randint(jax.random.fold_in(rng, axis), (), 0, dims[axis]) for axis in range(len(dims))]
    values = values.at[tuple(spot)].set(smallest)
    longest = dims.index(max(dims))
    spot[longest] = (spot[longest] + 1) % dims[longest]
    return values.at[tuple(spot)].set(high)


def shard_levels(stream_key, extent, cuts, smallest, high):
    factor_of, own = 1.0, jax.random.fold_in(stream_key, 6)
    for dim, blocks in cuts:
        heights = jnp.exp(jax.random.uniform(jax.random.fold_in(own, dim), (blocks,), jnp.float32, smallest / len(cuts), high / len(cuts)))
        factor_of = factor_of * jnp.repeat(heights, extent[dim] // blocks).reshape([-1 if axis == dim else 1 for axis in range(len(extent))])
    return factor_of


def setup_inputs(seed: int = 0) -> dict:
    key_list = jax.random.split(jax.random.key(seed), 6)
    return {
        "voltages": draw_voltages(jax.random.fold_in(key_list[5], 71), 0),
        "bandpass": jnp.clip(jnp.exp(math.log(3.0) - 2.3025851 * jax.random.uniform(key_list[1], (COARSE, NCH), jnp.float32) ** shard_levels(key_list[1], (COARSE, NCH), ((0, 4),), -0.2, 0.2)), 0.3, 3.0),
        "station_flags": place_ends((jax.random.randint(key_list[2], (STATIONS,), 0, 8) < 1).astype(jnp.int32), jax.random.fold_in(key_list[2], 1), 0, 1),
        "delays": place_ends(jax.random.randint(key_list[3], (BEAMS, STATIONS), 0, 4096), jax.random.fold_in(key_list[3], 1), 0, 4095).astype(jnp.int32),
        "section": draw_section(jax.random.fold_in(key_list[5], 71), 0),
    }


phase_period = 65536

def prototype():
    length = TAPS * NCH
    index = jnp.arange(length).astype(jnp.float32)
    offset = (index + 0.5 - length / 2.0) / NCH
    window = 0.5 - 0.5 * jnp.cos(2.0 * math.pi * (index + 0.5) / length)
    return (jnp.sinc(offset) * window).reshape(TAPS, NCH)

def filtered_frames(volt_block):
    framed = volt_block.astype(jnp.float32).reshape(2, STATIONS, POLS, FRAMES + TAPS - 1, NCH)
    tap_table = prototype()
    running = jnp.zeros((2, STATIONS, POLS, FRAMES, NCH), jnp.float32)
    for tap_index in range(TAPS):
        running = running + tap_table[tap_index] * framed[:, :, :, tap_index:tap_index + FRAMES, :]
    return running

def correlate(real_part, imag_part):
    input_arrays = STATIONS * POLS
    real_rows = real_part.reshape(input_arrays, FRAMES, VCH, AVG).transpose(2, 1, 3, 0).reshape(VCH, FRAMES * AVG, input_arrays)
    imag_rows = imag_part.reshape(input_arrays, FRAMES, VCH, AVG).transpose(2, 1, 3, 0).reshape(VCH, FRAMES * AVG, input_arrays)
    left_operand = jnp.concatenate([real_rows, imag_rows], axis=1)
    right_operand = jnp.concatenate([-imag_rows, real_rows], axis=1)
    upper = jnp.arange(input_arrays)[:, None] <= jnp.arange(input_arrays)[None, :]
    norm_scale = 1.0 / math.sqrt(FRAMES * AVG)

    def one_channel(pair):
        left_mat, right_mat = pair
        visibility_real = jnp.dot(left_mat.T, left_mat, preferred_element_type=jnp.float32)
        visibility_imaginary = jnp.dot(left_mat.T, right_mat, preferred_element_type=jnp.float32)
        return (jnp.where(upper, visibility_real, visibility_imaginary) * norm_scale).astype(jnp.bfloat16)
    return lax.map(one_channel, (left_operand, right_operand))

def beamform(real_part, imag_part, delays, coarse):
    real_blocks = real_part.reshape(STATIONS, POLS, FRAMES, VCH, AVG).transpose(3, 2, 0, 1, 4)
    imag_blocks = imag_part.reshape(STATIONS, POLS, FRAMES, VCH, AVG).transpose(3, 2, 0, 1, 4)
    norm_scale = 1.0 / math.sqrt(STATIONS)

    def one_block(items):
        block_index, real_blk, imag_blk = items
        frequency = (coarse * NCH + block_index * AVG + jnp.arange(AVG)).astype(jnp.int32)
        phase_index = delays[:, :, None] * frequency[None, None, :] % phase_period
        angle = 2.0 * math.pi * phase_index.astype(jnp.float32) / phase_period
        weight_real = jnp.cos(angle).astype(jnp.bfloat16).astype(jnp.float32)
        weight_imag = jnp.sin(angle).astype(jnp.bfloat16).astype(jnp.float32)
        real_f = real_blk.astype(jnp.float32)
        imag_f = imag_blk.astype(jnp.float32)
        out_real = jnp.einsum('bsj,mspj->jpmb', weight_real, real_f) - jnp.einsum('bsj,mspj->jpmb', weight_imag, imag_f)
        out_imag = jnp.einsum('bsj,mspj->jpmb', weight_real, imag_f) + jnp.einsum('bsj,mspj->jpmb', weight_imag, real_f)
        return (jnp.stack([out_real, out_imag], axis=1) * norm_scale).astype(jnp.bfloat16)
    block_ids = jnp.arange(VCH).astype(jnp.int32)
    result = lax.map(one_block, (block_ids, real_blocks, imag_blocks))
    return result.reshape(NCH, 2, POLS, FRAMES, BEAMS)

def reference(voltages, bandpass, station_flags, delays, section):
    spectra = []
    power_sum = jnp.zeros((STATIONS, POLS), jnp.float32)
    for coarse in range(COARSE):
        running = filtered_frames(voltages[:, :, coarse])
        spectrum = jnp.fft.fft(running[0] + 1j * running[1], axis=-1) * bandpass[coarse]
        spectra.append(spectrum)
        power_sum = power_sum + lax.optimization_barrier(jnp.sum(jnp.real(spectrum) ** 2 + jnp.imag(spectrum) ** 2, axis=(2, 3)))
    mean_power = power_sum / (COARSE * FRAMES * NCH)
    station_gain = jnp.where(station_flags[:, None] == 1, 0.0, 1.0 / jnp.sqrt(mean_power + 1e-05))
    vis_list = []
    beam_list = []
    input_arrays = STATIONS * POLS
    for coarse in range(COARSE):
        scaled = spectra[coarse] * station_gain[:, :, None, None]
        real_part = jnp.real(scaled).astype(jnp.bfloat16)
        imag_part = jnp.imag(scaled).astype(jnp.bfloat16)
        vis_list.append(lax.cond(section[coarse] == 0, lambda: correlate(real_part, imag_part), lambda: jnp.zeros((VCH, input_arrays, input_arrays), jnp.bfloat16)))
        beam_list.append(lax.cond(section[coarse] == 1, lambda: beamform(real_part, imag_part, delays, coarse), lambda: jnp.zeros((NCH, 2, POLS, FRAMES, BEAMS), jnp.bfloat16)))
    return (jnp.stack(vis_list), jnp.stack(beam_list))
```

```python
import functools
import math

import jax
import jax.numpy as jnp
import numpy as np
from jax import lax
from jax.experimental import pallas as pl
from jax.experimental.pallas import tpu as pltpu
from jax.sharding import PartitionSpec as P

POLS = 2
NCH = 6144
TAPS = 8
FRAMES = 6
AVG = 12
BEAMS = 256
STATIONS = 128
INPUTS = STATIONS * POLS
PER_GROUP = 48
VIS_LOCAL = PER_GROUP // AVG
BLOCK = AVG * 2 * FRAMES
PERIOD = 65536
GAIN_LANE = 64

NT = (((1,), (1,)), ((), ()))
NN = (((1,), (0,)), ((), ()))


def dot_f32(lhs, rhs, dims):
    return lax.dot_general(lhs, rhs, dims, preferred_element_type=jnp.float32)


def swap_table():
    table = np.zeros((VIS_LOCAL, INPUTS, INPUTS), np.float32)
    for v in range(VIS_LOCAL):
        for q in range(BLOCK):
            real = q % 12 < 6
            table[v, 16 * v + q, 16 * v + (q + 6 if real else q - 6)] = -1.0 if real else 1.0
    return table


def split_table():
    table = np.zeros((INPUTS, INPUTS), np.float32)
    for pol in range(POLS):
        for station in range(STATIONS):
            table[pol * STATIONS + station, station * POLS + pol] = 1.0
    return table


def finish_kernel(
    scal_ref, delays_ref, r_ref, swap_ref, split_ref, vis_ref, beam_ref, xl_ref, xs_ref, w_ref
):
    is_beam = scal_ref[0] == 1

    @pl.when(jnp.logical_not(is_beam))
    def _():
        beam_ref[...] = jnp.zeros_like(beam_ref)
        last = r_ref[VIS_LOCAL]
        gain_col = jnp.sum(
            last[:, GAIN_LANE : GAIN_LANE + 3].astype(jnp.float32), axis=1, keepdims=True
        )
        gain_col = gain_col * (1.0 / math.sqrt(FRAMES * AVG))
        lane8 = lax.broadcasted_iota(jnp.int32, (8, 128), 1)
        pick = jnp.where((lane8 >= GAIN_LANE) & (lane8 < GAIN_LANE + 3), 1.0, 0.0)
        gain_row = dot_f32(pick.astype(jnp.bfloat16), last, NT)[0:1, :]
        rows = lax.broadcasted_iota(jnp.int32, (INPUTS, INPUTS), 0)
        cols = lax.broadcasted_iota(jnp.int32, (INPUTS, INPUTS), 1)
        for v in range(VIS_LOCAL):
            left = jnp.concatenate([r_ref[v], r_ref[v + 1]], axis=1)
            inside = (cols >= 16 * v) & (cols < 16 * v + BLOCK)
            same = jnp.where(inside, left.astype(jnp.float32), 0.0).astype(jnp.bfloat16)
            other = dot_f32(left, swap_ref[v], NT).astype(jnp.bfloat16)
            real = dot_f32(left, same, NT)
            imag = dot_f32(left, other, NT)
            packed = jnp.where(rows <= cols, real, imag)
            vis_ref[v] = (packed * gain_col * gain_row).astype(jnp.bfloat16)

    @pl.when(is_beam)
    def _():
        vis_ref[...] = jnp.zeros_like(vis_ref)
        first = scal_ref[1]
        delay = delays_ref[...].astype(jnp.float32).T.astype(jnp.int32)
        turn = 2.0 * math.pi / PERIOD
        start = (delay * first & (PERIOD - 1)).astype(jnp.float32) * turn
        step = delay.astype(jnp.float32) * turn
        w_state = (jnp.cos(start), jnp.sin(start), jnp.cos(step), jnp.sin(step))
        for sb in range(8):
            band = slice(16 * sb, 16 * sb + 16)
            cs, sn, dc, ds = (t[band] for t in w_state)

            def advance(k, carry):
                c, s = carry
                w_ref[k, 16 * sb : 16 * sb + 16, :] = c.astype(jnp.bfloat16)
                w_ref[k, 128 + 16 * sb : 128 + 16 * sb + 16, :] = s.astype(jnp.bfloat16)
                return (c * dc - s * ds, c * ds + s * dc)

            lax.fori_loop(0, PER_GROUP, advance, (cs, sn), unroll=4)

        gain = None
        for j in range(VIS_LOCAL, -1, -1):
            part = dot_f32(split_ref[...], r_ref[j], NN)
            if gain is None:
                gain = jnp.sum(part[:, GAIN_LANE : GAIN_LANE + 3], axis=1, keepdims=True)
            xs_ref[j] = (part * gain).astype(jnp.bfloat16)
        q_row = lax.broadcasted_iota(jnp.int32, (BLOCK, INPUTS), 0)
        q_col = lax.broadcasted_iota(jnp.int32, (BLOCK, INPUTS), 1)
        for v in range(VIS_LOCAL):
            window = jnp.concatenate([xs_ref[v], xs_ref[v + 1]], axis=1)
            keep = jnp.where(q_col == q_row + 16 * v, 1.0, 0.0).astype(jnp.bfloat16)
            plain = dot_f32(keep, window, NT)
            other = dot_f32(swap_ref[v, 16 * v : 16 * v + BLOCK, :], window, NT)
            for pol in range(POLS):
                rows = pl.ds(2 * BLOCK * v + pol, BLOCK, stride=2)
                half = slice(128 * pol, 128 * pol + 128)
                xl_ref[0, rows, :] = plain[:, half]
                xl_ref[1, rows, :] = other[:, half]
        scale = 1.0 / math.sqrt(STATIONS)

        def one_channel(k, carry):
            rows = pl.ds(pl.multiple_of(24 * k, 8), 24)
            left = jnp.concatenate([xl_ref[0, rows, :], xl_ref[1, rows, :]], axis=1)
            out = dot_f32(left.astype(jnp.bfloat16), w_ref[k], NN) * scale
            beam_ref[k] = out.astype(jnp.bfloat16).reshape(2 * FRAMES, POLS, BEAMS)
            return carry

        lax.fori_loop(0, PER_GROUP, one_channel, 0, unroll=4)


def finish(scal, delays, received):
    vmem = pl.BlockSpec(memory_space=pltpu.VMEM)
    vis, beam = pl.pallas_call(
        finish_kernel,
        out_shape=(
            jax.ShapeDtypeStruct((VIS_LOCAL, INPUTS, INPUTS), jnp.bfloat16),
            jax.ShapeDtypeStruct((PER_GROUP, 2 * FRAMES, POLS, BEAMS), jnp.bfloat16),
        ),
        in_specs=[pl.BlockSpec(memory_space=pltpu.SMEM)] + [vmem] * 4,
        out_specs=(vmem, vmem),
        scratch_shapes=[
            pltpu.VMEM((2, PER_GROUP * 24, 128), jnp.float32),
            pltpu.VMEM((5, INPUTS, 128), jnp.bfloat16),
            pltpu.VMEM((PER_GROUP, INPUTS, BEAMS), jnp.bfloat16),
        ],
        name="finish",
    )(
        scal,
        delays,
        received,
        jnp.asarray(swap_table(), jnp.bfloat16),
        jnp.asarray(split_table(), jnp.bfloat16),
    )
    tied = beam.reshape(PER_GROUP, 2, FRAMES, POLS, BEAMS).transpose(0, 1, 3, 2, 4)
    return vis, tied


def prototype():
    length = TAPS * NCH
    index = jnp.arange(length).astype(jnp.float32)
    offset = (index + 0.5 - length / 2.0) / NCH
    window = 0.5 - 0.5 * jnp.cos(2.0 * math.pi * (index + 0.5) / length)
    return (jnp.sinc(offset) * window).reshape(TAPS, NCH)


def dft_table(count_rows, count_cols, modulus):
    row_ids = jnp.arange(count_rows)[:, None]
    col_ids = jnp.arange(count_cols)[None, :]
    angle = 2.0 * math.pi * (row_ids * col_ids % modulus).astype(jnp.float32) / modulus
    return (jnp.cos(angle), -jnp.sin(angle))


def fourier_transform(real_in, imag_in):
    leading = real_in.shape[:-1]
    length = real_in.shape[-1]
    inner_len = 128
    outer_len = length // inner_len
    high = lax.Precision.HIGH
    real_grid = real_in.reshape(leading + (outer_len, inner_len))
    imag_grid = imag_in.reshape(leading + (outer_len, inner_len))
    cos_outer, outer_sine = dft_table(outer_len, outer_len, outer_len)
    segment_real = jnp.einsum("...ai,ak->...ki", real_grid, cos_outer, precision=high) - jnp.einsum(
        "...ai,ak->...ki", imag_grid, outer_sine, precision=high
    )
    segment_imag = jnp.einsum(
        "...ai,ak->...ki", real_grid, outer_sine, precision=high
    ) + jnp.einsum("...ai,ak->...ki", imag_grid, cos_outer, precision=high)
    cos_twist, sin_twist = dft_table(outer_len, inner_len, length)
    twist_real = segment_real * cos_twist - segment_imag * sin_twist
    twist_imag = segment_real * sin_twist + segment_imag * cos_twist
    cos_inner, sin_inner = dft_table(inner_len, inner_len, inner_len)
    out_real = jnp.einsum("...ki,il->...kl", twist_real, cos_inner, precision=high) - jnp.einsum(
        "...ki,il->...kl", twist_imag, sin_inner, precision=high
    )
    out_imag = jnp.einsum("...ki,il->...kl", twist_real, sin_inner, precision=high) + jnp.einsum(
        "...ki,il->...kl", twist_imag, cos_inner, precision=high
    )
    out_real = jnp.swapaxes(out_real, -1, -2).reshape(leading + (length,))
    out_imag = jnp.swapaxes(out_imag, -1, -2).reshape(leading + (length,))
    return (out_real, out_imag)


def per_device(voltages, bandpass, station_flags, delays, section):
    stn_count = lax.axis_size("stn")
    sec_count = lax.axis_size("sec")
    local_stations = voltages.shape[1]
    framed = voltages[:, :, 0].reshape(2, local_stations, POLS, FRAMES + TAPS - 1, NCH)
    tap_table = prototype()
    filtered_sum = jnp.zeros((2, local_stations, POLS, FRAMES, NCH), jnp.float32)
    for tap_index in range(TAPS):
        filtered_sum = (
            filtered_sum + tap_table[tap_index] * framed[:, :, :, tap_index : tap_index + FRAMES, :]
        )
    spec_real, spec_imag = fourier_transform(filtered_sum[0], filtered_sum[1])
    spec_real = spec_real * bandpass[0]
    spec_imag = spec_imag * bandpass[0]
    local_power = jnp.sum(spec_real * spec_real + spec_imag * spec_imag, axis=(2, 3))
    power_sum = lax.psum(local_power, "sec")
    mean_power = power_sum / (sec_count * FRAMES * NCH)
    station_gain = jnp.where(station_flags[:, None] == 1, 0.0, 1.0 / jnp.sqrt(mean_power + 1e-05))
    norm_real = (spec_real * station_gain[:, :, None, None]).astype(jnp.bfloat16)
    norm_imag = (spec_imag * station_gain[:, :, None, None]).astype(jnp.bfloat16)
    parts = jnp.stack([norm_real[0], norm_imag[0]])
    parts = parts.reshape(2, POLS, FRAMES, stn_count, PER_GROUP).transpose(3, 1, 4, 0, 2)
    message = parts.reshape(stn_count, POLS, PER_GROUP * 2 * FRAMES)
    tail = jnp.zeros((stn_count, POLS, 64), jnp.bfloat16).at[:, :, 0].set(1.0)
    message = jnp.concatenate([message, tail], axis=2)
    turned = lax.all_to_all(message, "stn", split_axis=0, concat_axis=0, tiled=True)
    received = turned.reshape(INPUTS, 5, 128).transpose(1, 0, 2)
    coarse = lax.axis_index("sec")
    first = coarse * NCH + lax.axis_index("stn") * PER_GROUP
    scal = jnp.stack([section[coarse], first]).astype(jnp.int32)
    vis, tied = finish(scal, delays, received)
    return (vis[None], tied[None])


def solution(mesh):
    return jax.shard_map(
        per_device,
        mesh=mesh,
        in_specs=(P(None, "stn", "sec", None, None), P("sec", None), P("stn"), P(), P()),
        out_specs=(P("sec", "stn", None, None), P("sec", "stn", None, None, None, None)),
        check_vma=False,
    )
```

```python
import functools
import math

import jax
import jax.numpy as jnp
import numpy as np
from jax import lax
from jax.experimental import pallas as pl
from jax.experimental.pallas import tpu as pltpu
from jax.sharding import PartitionSpec as P

POLS = 2
NCH = 6144
TAPS = 8
FRAMES = 6
AVG = 12
BEAMS = 256
STATIONS = 128
INPUTS = STATIONS * POLS
PER_GROUP = 48
VIS_LOCAL = PER_GROUP // AVG
BLOCK = AVG * 2 * FRAMES
PERIOD = 65536
GAIN_LANE = 64

NT = (((1,), (1,)), ((), ()))
NN = (((1,), (0,)), ((), ()))


def dot_f32(lhs, rhs, dims):
    return lax.dot_general(lhs, rhs, dims, preferred_element_type=jnp.float32)


def swap_table():
    table = np.zeros((VIS_LOCAL, INPUTS, INPUTS), np.float32)
    for v in range(VIS_LOCAL):
        for q in range(BLOCK):
            real = q % 12 < 6
            table[v, 16 * v + q, 16 * v + (q + 6 if real else q - 6)] = -1.0 if real else 1.0
    return table


def split_table():
    table = np.zeros((INPUTS, INPUTS), np.float32)
    for pol in range(POLS):
        for station in range(STATIONS):
            table[pol * STATIONS + station, station * POLS + pol] = 1.0
    return table


def finish_kernel(
    scal_ref, delays_ref, r_ref, swap_ref, split_ref, vis_ref, beam_ref, xl_ref, xs_ref, w_ref
):
    is_beam = scal_ref[0] == 1

    @pl.when(jnp.logical_not(is_beam))
    def _():
        beam_ref[...] = jnp.zeros_like(beam_ref)
        last = r_ref[VIS_LOCAL]
        gain_col = jnp.sum(
            last[:, GAIN_LANE : GAIN_LANE + 3].astype(jnp.float32), axis=1, keepdims=True
        )
        gain_col = gain_col * (1.0 / math.sqrt(FRAMES * AVG))
        lane8 = lax.broadcasted_iota(jnp.int32, (8, 128), 1)
        pick = jnp.where((lane8 >= GAIN_LANE) & (lane8 < GAIN_LANE + 3), 1.0, 0.0)
        gain_row = dot_f32(pick.astype(jnp.bfloat16), last, NT)[0:1, :]
        rows = lax.broadcasted_iota(jnp.int32, (INPUTS, INPUTS), 0)
        cols = lax.broadcasted_iota(jnp.int32, (INPUTS, INPUTS), 1)
        for v in range(VIS_LOCAL):
            left = jnp.concatenate([r_ref[v], r_ref[v + 1]], axis=1)
            inside = (cols >= 16 * v) & (cols < 16 * v + BLOCK)
            same = jnp.where(inside, left.astype(jnp.float32), 0.0).astype(jnp.bfloat16)
            other = dot_f32(left, swap_ref[v], NT).astype(jnp.bfloat16)
            real = dot_f32(left, same, NT)
            imag = dot_f32(left, other, NT)
            packed = jnp.where(rows <= cols, real, imag)
            vis_ref[v] = (packed * gain_col * gain_row).astype(jnp.bfloat16)

    @pl.when(is_beam)
    def _():
        vis_ref[...] = jnp.zeros_like(vis_ref)
        first = scal_ref[1]
        delay = delays_ref[...].astype(jnp.float32).T.astype(jnp.int32)
        turn = 2.0 * math.pi / PERIOD
        start = (delay * first & (PERIOD - 1)).astype(jnp.float32) * turn
        step = delay.astype(jnp.float32) * turn
        w_state = (jnp.cos(start), jnp.sin(start), jnp.cos(step), jnp.sin(step))
        for sb in range(8):
            band = slice(16 * sb, 16 * sb + 16)
            cs, sn, dc, ds = (t[band] for t in w_state)

            def advance(k, carry):
                c, s = carry
                w_ref[k, 16 * sb : 16 * sb + 16, :] = c.astype(jnp.bfloat16)
                w_ref[k, 128 + 16 * sb : 128 + 16 * sb + 16, :] = s.astype(jnp.bfloat16)
                return (c * dc - s * ds, c * ds + s * dc)

            lax.fori_loop(0, PER_GROUP, advance, (cs, sn), unroll=4)

        gain = None
        for j in range(VIS_LOCAL, -1, -1):
            part = dot_f32(split_ref[...], r_ref[j], NN)
            if gain is None:
                gain = jnp.sum(part[:, GAIN_LANE : GAIN_LANE + 3], axis=1, keepdims=True)
            xs_ref[j] = (part * gain).astype(jnp.bfloat16)
        q_row = lax.broadcasted_iota(jnp.int32, (BLOCK, INPUTS), 0)
        q_col = lax.broadcasted_iota(jnp.int32, (BLOCK, INPUTS), 1)
        for v in range(VIS_LOCAL):
            window = jnp.concatenate([xs_ref[v], xs_ref[v + 1]], axis=1)
            keep = jnp.where(q_col == q_row + 16 * v, 1.0, 0.0).astype(jnp.bfloat16)
            plain = dot_f32(keep, window, NT)
            other = dot_f32(swap_ref[v, 16 * v : 16 * v + BLOCK, :], window, NT)
            for pol in range(POLS):
                rows = pl.ds(2 * BLOCK * v + pol, BLOCK, stride=2)
                half = slice(128 * pol, 128 * pol + 128)
                xl_ref[0, rows, :] = plain[:, half]
                xl_ref[1, rows, :] = other[:, half]
        scale = 1.0 / math.sqrt(STATIONS)

        def one_channel(k, carry):
            rows = pl.ds(pl.multiple_of(24 * k, 8), 24)
            left = jnp.concatenate([xl_ref[0, rows, :], xl_ref[1, rows, :]], axis=1)
            out = dot_f32(left.astype(jnp.bfloat16), w_ref[k], NN) * scale
            beam_ref[k] = out.astype(jnp.bfloat16).reshape(2 * FRAMES, POLS, BEAMS)
            return carry

        lax.fori_loop(0, PER_GROUP, one_channel, 0, unroll=4)


def finish(scal, delays, received):
    vmem = pl.BlockSpec(memory_space=pltpu.VMEM)
    vis, beam = pl.pallas_call(
        finish_kernel,
        out_shape=(
            jax.ShapeDtypeStruct((VIS_LOCAL, INPUTS, INPUTS), jnp.bfloat16),
            jax.ShapeDtypeStruct((PER_GROUP, 2 * FRAMES, POLS, BEAMS), jnp.bfloat16),
        ),
        in_specs=[pl.BlockSpec(memory_space=pltpu.SMEM)] + [vmem] * 4,
        out_specs=(vmem, vmem),
        scratch_shapes=[
            pltpu.VMEM((2, PER_GROUP * 24, 128), jnp.float32),
            pltpu.VMEM((5, INPUTS, 128), jnp.bfloat16),
            pltpu.VMEM((PER_GROUP, INPUTS, BEAMS), jnp.bfloat16),
        ],
        name="finish",
    )(
        scal,
        delays,
        received,
        jnp.asarray(swap_table(), jnp.bfloat16),
        jnp.asarray(split_table(), jnp.bfloat16),
    )
    tied = beam.reshape(PER_GROUP, 2, FRAMES, POLS, BEAMS).transpose(0, 1, 3, 2, 4)
    return vis, tied


def split2(value):
    high = value.astype(jnp.bfloat16)
    return high, (value - high.astype(jnp.float32)).astype(jnp.bfloat16)


def split_const(table):
    table = np.asarray(table, np.float32)
    high = table.astype(jnp.bfloat16)
    return high, (table - high.astype(np.float32)).astype(jnp.bfloat16)


def taper_table():
    index = np.arange(TAPS * NCH, dtype=np.float64)
    offset = (index + 0.5 - TAPS * NCH / 2.0) / NCH
    window = 0.5 - 0.5 * np.cos(2.0 * np.pi * (index + 0.5) / (TAPS * NCH))
    table = (np.sinc(offset) * window).reshape(TAPS, PER_GROUP, 1, 128)
    table = np.broadcast_to(table, (TAPS, PER_GROUP, POLS, 128))
    return table.reshape(TAPS, 2 * PER_GROUP, 128).astype(np.float32)


def outer_table():
    angle = 2.0 * np.pi * (np.outer(np.arange(48), np.arange(48)) % 48) / 48.0
    cos, sin = np.cos(angle), np.sin(angle)
    table = np.zeros((POLS, 2, 48, 2, 48, POLS))
    for pol in range(POLS):
        table[pol, 0, :, 0, :, pol] = cos
        table[pol, 0, :, 1, :, pol] = sin
        table[pol, 1, :, 0, :, pol] = -sin
        table[pol, 1, :, 1, :, pol] = cos
    return table.reshape(192, 192)


def twist_tables():
    angle = 2.0 * np.pi * np.outer(np.arange(48), np.arange(128)) / NCH
    return np.stack([np.cos(angle), np.sin(angle)]).astype(np.float32)


def inner_table():
    angle = 2.0 * np.pi * (np.outer(np.arange(128), np.arange(128)) % 128) / 128.0
    return np.concatenate([np.cos(angle), np.sin(angle)], axis=1)


def spread_table():
    table = np.zeros((48, 640), np.float32)
    for k1 in range(48):
        table[k1, 12 * k1 : 12 * k1 + 12] = 1.0
    return np.concatenate([table] * 3, axis=0)


def channelize_kernel(
    flag_ref,
    volt_ref,
    band_ref,
    taper_ref,
    outer_h_ref,
    outer_l_ref,
    twist_ref,
    inner_h_ref,
    inner_l_ref,
    spread_ref,
    recv_ref,
    fh_ref,
    fl_ref,
    y_ref,
    o_ref,
    send_ref,
    pow_ref,
    send_sem,
    recv_sem,
    own_sem,
):
    stn_count, sec_count = STATIONS, 4
    me, sec = lax.axis_index("stn"), lax.axis_index("sec")
    barrier = pltpu.get_barrier_semaphore()

    def partner(j):
        return lax.rem(me + lax.rem(j * 37, stn_count), stn_count)

    def greet(j, carry):
        pl.semaphore_signal(barrier, inc=1, device_id=(partner(j), sec), device_id_type=MESH)
        return carry

    lax.fori_loop(1, stn_count, greet, 0)
    for j in range(1, sec_count):
        other = lax.rem(sec + j, sec_count)
        pl.semaphore_signal(barrier, inc=1, device_id=(me, other), device_id_type=MESH)

    for part in range(2):
        for chunk in range(6):
            rows = slice(16 * chunk, 16 * chunk + 16)
            taps = [taper_ref[j, rows, :] for j in range(TAPS)]
            blocks = [
                volt_ref[part, 96 * n + 16 * chunk : 96 * n + 16 * chunk + 16, :].astype(jnp.float32)
                for n in range(FRAMES + TAPS - 1)
            ]
            for m in range(FRAMES):
                total = taps[0] * blocks[m]
                for j in range(1, TAPS):
                    total = total + taps[j] * blocks[m + j]
                high, low = split2(total)
                at = slice(96 * part + 16 * chunk, 96 * part + 16 * chunk + 16)
                fh_ref[at, 128 * m : 128 * m + 128] = high
                fl_ref[at, 128 * m : 128 * m + 128] = low

    cos, sin = twist_ref[0], twist_ref[1]
    for pair in range(FRAMES // 2):
        lanes = slice(256 * pair, 256 * pair + 256)
        fh = fh_ref[:, lanes]
        seg = dot_f32(outer_h_ref[...], fh, NN)
        seg = seg + dot_f32(outer_l_ref[...], fh, NN)
        seg = seg + dot_f32(outer_h_ref[...], fl_ref[:, lanes], NN)
        for half in range(2):
            m = 2 * pair + half
            for pol in range(POLS):
                sr = seg[96 * pol : 96 * pol + 48, 128 * half : 128 * half + 128]
                si = seg[96 * pol + 48 : 96 * pol + 96, 128 * half : 128 * half + 128]
                yr = sr * cos + si * sin
                yi = si * cos - sr * sin
                real_rows = pl.ds(m, 48, stride=12)
                imag_rows = pl.ds(FRAMES + m, 48, stride=12)
                y_ref[2 * pol, real_rows, :] = yr
                y_ref[2 * pol + 1, real_rows, :] = yi
                y_ref[2 * pol, imag_rows, :] = yi
                y_ref[2 * pol + 1, imag_rows, :] = -yr

    band = band_ref[...]
    b0 = band.astype(jnp.bfloat16)
    rest = band - b0.astype(jnp.float32)
    b1 = rest.astype(jnp.bfloat16)
    b2 = (rest - b1.astype(jnp.float32)).astype(jnp.bfloat16)
    parts = [b.astype(jnp.float32) for b in (b0, b1, b2)]
    band3 = jnp.concatenate(parts, axis=1).astype(jnp.bfloat16)
    powers = [jnp.zeros((8, 128), jnp.float32) for _ in range(POLS)]
    for first, count in ((0, 2), (2, 2), (4, 1)):
        width = 128 * count
        depth = min(width, 576 - 128 * first)
        spread = dot_f32(band3, spread_ref[:, 128 * first : 128 * first + width], NN)
        for pol in range(POLS):
            y = jnp.concatenate(
                [y_ref[2 * pol + t, 128 * first : 128 * first + depth, :] for t in range(2)], axis=1
            )
            if depth < width:
                y = jnp.concatenate([y, jnp.zeros((width - depth, 256), jnp.float32)], axis=0)
            yh, yl = split2(y)
            out = dot_f32(inner_h_ref[...], yh, NT)
            out = out + dot_f32(inner_l_ref[...], yh, NT)
            out = out + dot_f32(inner_h_ref[...], yl, NT)
            out = out * spread
            square = out * out
            for t in range(count):
                piece = slice(128 * t, 128 * t + 128)
                o_ref[first + t, pl.ds(pol, 128, stride=2), :] = out[:, piece]
                powers[pol] = powers[pol] + jnp.sum(square[:, piece].reshape(16, 8, 128), axis=0)
    for j in range(4):
        send_ref[j] = o_ref[j].astype(jnp.bfloat16).reshape(128, 2, 128)
    lane = lax.broadcasted_iota(jnp.int32, (1, 128), 1)
    totals = [jnp.sum(p, keepdims=True) for p in powers]
    pow_ref[sec_count] = jnp.where(lane < 64, totals[0], totals[1])

    pl.semaphore_wait(barrier, stn_count - 1 + sec_count - 1)

    def power_copy(j):
        other = lax.rem(sec + j, sec_count)
        return pltpu.make_async_remote_copy(
            src_ref=pow_ref.at[sec_count],
            dst_ref=pow_ref.at[sec],
            send_sem=send_sem.at[0],
            recv_sem=recv_sem.at[0],
            device_id=(me, other),
            device_id_type=MESH,
        )

    for j in range(1, sec_count):
        power_copy(j).start()

    def block_copy(j, tiles, slot):
        to = partner(j)
        return pltpu.make_async_remote_copy(
            src_ref=send_ref.at[tiles, to],
            dst_ref=recv_ref.at[tiles, me],
            send_sem=send_sem.at[slot],
            recv_sem=recv_sem.at[slot],
            device_id=(to, sec),
            device_id_type=MESH,
        )

    body, tail = pl.ds(0, 4), pl.ds(4, 1)

    def send_body(j, carry):
        block_copy(j, body, 1).start()
        return carry

    lax.fori_loop(1, stn_count, send_body, 0)

    def bytes_of(ref, slot):
        return pltpu.make_async_remote_copy(
            src_ref=ref,
            dst_ref=ref,
            send_sem=send_sem.at[slot],
            recv_sem=recv_sem.at[slot],
            device_id=(me, sec),
            device_id_type=MESH,
        )

    three = bytes_of(pow_ref.at[pl.ds(0, sec_count - 1)], 0)
    three.wait_send()
    three.wait_recv()
    mine = lax.broadcasted_iota(jnp.int32, (1, 128), 1) * 0 + sec
    total = pow_ref[sec_count]
    for other in range(sec_count):
        total = total + jnp.where(mine == other, 0.0, pow_ref[other])
    mean = total * (1.0 / (sec_count * FRAMES * NCH))
    gain = jnp.where(flag_ref[0] == 1, 0.0, 1.0 / jnp.sqrt(mean + 1e-05))
    g0 = gain.astype(jnp.bfloat16).astype(jnp.float32)
    g1 = (gain - g0).astype(jnp.bfloat16).astype(jnp.float32)
    g2 = gain - g0 - g1
    row = lax.broadcasted_iota(jnp.int32, (256, 128), 0)
    col = lax.broadcasted_iota(jnp.int32, (256, 128), 1)
    tile = o_ref[4]
    for at, g in ((0, g0), (1, g1), (2, g2)):
        pair = jnp.where(row % 2 == 0, g[:, 0:1], g[:, 64:65])
        tile = jnp.where(col == GAIN_LANE + at, pair, tile)
    send_ref[4] = tile.astype(jnp.bfloat16).reshape(128, 2, 128)

    def send_tail(j, carry):
        block_copy(j, tail, 2).start()
        return carry

    lax.fori_loop(1, stn_count, send_tail, 0)
    own = pltpu.make_async_copy(send_ref.at[:, me], recv_ref.at[:, me], own_sem)
    own.start()
    own.wait()
    for tiles, slot in ((body, 1), (tail, 2)):
        whole = bytes_of(send_ref.at[tiles, pl.ds(0, stn_count - 1)], slot)
        whole.wait_send()
        landed = bytes_of(recv_ref.at[tiles, pl.ds(0, stn_count - 1)], slot)
        landed.wait_recv()


MESH = pl.DeviceIdType.MESH


def channelize(flags, volts, band):
    vmem = pl.BlockSpec(memory_space=pltpu.VMEM)
    outer_h, outer_l = split_const(outer_table())
    inner_h, inner_l = split_const(inner_table())
    return pl.pallas_call(
        channelize_kernel,
        out_shape=jax.ShapeDtypeStruct((5, STATIONS, POLS, 128), jnp.bfloat16),
        in_specs=[pl.BlockSpec(memory_space=pltpu.SMEM)] + [vmem] * 9,
        out_specs=pl.BlockSpec(memory_space=pl.ANY),
        scratch_shapes=[
            pltpu.VMEM((192, 768), jnp.bfloat16),
            pltpu.VMEM((192, 768), jnp.bfloat16),
            pltpu.VMEM((4, 576, 128), jnp.float32),
            pltpu.VMEM((5, 256, 128), jnp.float32),
            pltpu.VMEM((5, STATIONS, POLS, 128), jnp.bfloat16),
            pltpu.VMEM((5, 1, 128), jnp.float32),
            pltpu.SemaphoreType.DMA((3,)),
            pltpu.SemaphoreType.DMA((3,)),
            pltpu.SemaphoreType.DMA,
        ],
        compiler_params=pltpu.CompilerParams(collective_id=0, has_side_effects=True),
        name="channelize",
    )(
        flags,
        volts,
        band,
        jnp.asarray(taper_table()),
        jnp.asarray(outer_h),
        jnp.asarray(outer_l),
        jnp.asarray(twist_tables()),
        jnp.asarray(inner_h),
        jnp.asarray(inner_l),
        jnp.asarray(spread_table(), jnp.bfloat16),
    )


def per_device(voltages, bandpass, station_flags, delays, section):
    volts = voltages.reshape(2, POLS, 624, 128).transpose(0, 2, 1, 3).reshape(2, 1248, 128)
    band = bandpass.reshape(STATIONS, PER_GROUP)
    turned = channelize(station_flags, volts, band)
    received = turned.reshape(5, INPUTS, 128)
    coarse = lax.axis_index("sec")
    first = coarse * NCH + lax.axis_index("stn") * PER_GROUP
    scal = jnp.stack([section[coarse], first]).astype(jnp.int32)
    vis, tied = finish(scal, delays, received)
    return (vis[None], tied[None])


def solution(mesh):
    return jax.shard_map(
        per_device,
        mesh=mesh,
        in_specs=(P(None, "stn", "sec", None, None), P("sec", None), P("stn"), P(), P()),
        out_specs=(P("sec", "stn", None, None), P("sec", "stn", None, None, None, None)),
        check_vma=False,
    )
```

```python
import functools
import math

import jax
import jax.numpy as jnp
import numpy as np
from jax import lax
from jax.experimental import pallas as pl
from jax.experimental.pallas import tpu as pltpu
from jax.sharding import PartitionSpec as P

POLS = 2
NCH = 6144
TAPS = 8
FRAMES = 6
AVG = 12
BEAMS = 256
STATIONS = 128
INPUTS = STATIONS * POLS
PER_GROUP = 48
VIS_LOCAL = PER_GROUP // AVG
BLOCK = AVG * 2 * FRAMES
PERIOD = 65536
GAIN_LANE = 64
W_CHUNKS = 8
W_STEP = PER_GROUP // W_CHUNKS
PLANES = 8
PLANE = STATIONS // PLANES
SECTIONS = 4
MESH = pl.DeviceIdType.MESH

NT = (((1,), (1,)), ((), ()))
NN = (((1,), (0,)), ((), ()))


def dot_f32(lhs, rhs, dims):
    return lax.dot_general(lhs, rhs, dims, preferred_element_type=jnp.float32)


def swap_table():
    table = np.zeros((VIS_LOCAL, INPUTS, INPUTS), np.float32)
    for v in range(VIS_LOCAL):
        for q in range(BLOCK):
            real = q % 12 < 6
            table[v, 16 * v + q, 16 * v + (q + 6 if real else q - 6)] = -1.0 if real else 1.0
    return table


def split_table():
    table = np.zeros((INPUTS, INPUTS), np.float32)
    for pol in range(POLS):
        for station in range(STATIONS):
            table[pol * STATIONS + station, station * POLS + pol] = 1.0
    return table


def finish_kernel(
    section_ref,
    w_hbm_ref,
    r_ref,
    swap_ref,
    split_ref,
    vis_ref,
    beam_ref,
    xl_ref,
    xs_ref,
    w_ref,
    w_sem,
):
    is_beam = section_ref[lax.axis_index("sec")] == 1

    @pl.when(jnp.logical_not(is_beam))
    def _():
        beam_ref[...] = jnp.zeros_like(beam_ref)
        last = r_ref[VIS_LOCAL]
        gain_col = jnp.sum(
            last[:, GAIN_LANE : GAIN_LANE + 3].astype(jnp.float32), axis=1, keepdims=True
        )
        gain_col = gain_col * (1.0 / math.sqrt(FRAMES * AVG))
        lane8 = lax.broadcasted_iota(jnp.int32, (8, 128), 1)
        pick = jnp.where((lane8 >= GAIN_LANE) & (lane8 < GAIN_LANE + 3), 1.0, 0.0)
        gain_row = dot_f32(pick.astype(jnp.bfloat16), last, NT)[0:1, :]
        rows = lax.broadcasted_iota(jnp.int32, (INPUTS, INPUTS), 0)
        cols = lax.broadcasted_iota(jnp.int32, (INPUTS, INPUTS), 1)
        for v in range(VIS_LOCAL):
            left = jnp.concatenate([r_ref[v], r_ref[v + 1]], axis=1)
            inside = (cols >= 16 * v) & (cols < 16 * v + BLOCK)
            same = jnp.where(inside, left.astype(jnp.float32), 0.0).astype(jnp.bfloat16)
            other = dot_f32(left, swap_ref[v], NT).astype(jnp.bfloat16)
            real = dot_f32(left, same, NT)
            imag = dot_f32(left, other, NT)
            packed = jnp.where(rows <= cols, real, imag)
            vis_ref[v] = (packed * gain_col * gain_row).astype(jnp.bfloat16)

    @pl.when(is_beam)
    def _():
        copies = []
        for n in range(W_CHUNKS):
            part = pl.ds(W_STEP * n, W_STEP)
            copies.append(
                pltpu.make_async_copy(w_hbm_ref.at[part], w_ref.at[part], w_sem.at[n])
            )
            copies[n].start()
        vis_ref[...] = jnp.zeros_like(vis_ref)
        gain = None
        for j in range(VIS_LOCAL, -1, -1):
            part = dot_f32(split_ref[...], r_ref[j], NN)
            if gain is None:
                gain = jnp.sum(part[:, GAIN_LANE : GAIN_LANE + 3], axis=1, keepdims=True)
            xs_ref[j] = (part * gain).astype(jnp.bfloat16)
        q_row = lax.broadcasted_iota(jnp.int32, (BLOCK, INPUTS), 0)
        q_col = lax.broadcasted_iota(jnp.int32, (BLOCK, INPUTS), 1)
        for v in range(VIS_LOCAL):
            window = jnp.concatenate([xs_ref[v], xs_ref[v + 1]], axis=1)
            keep = jnp.where(q_col == q_row + 16 * v, 1.0, 0.0).astype(jnp.bfloat16)
            plain = dot_f32(keep, window, NT)
            other = dot_f32(swap_ref[v, 16 * v : 16 * v + BLOCK, :], window, NT)
            for pol in range(POLS):
                rows = pl.ds(2 * BLOCK * v + pol, BLOCK, stride=2)
                half = slice(128 * pol, 128 * pol + 128)
                xl_ref[0, rows, :] = plain[:, half]
                xl_ref[1, rows, :] = other[:, half]
        scale = 1.0 / math.sqrt(STATIONS)

        def one_channel(k, carry):
            rows = pl.ds(pl.multiple_of(24 * k, 8), 24)
            left = jnp.concatenate([xl_ref[0, rows, :], xl_ref[1, rows, :]], axis=1)
            out = dot_f32(left.astype(jnp.bfloat16), w_ref[k], NN) * scale
            beam_ref[k] = out.astype(jnp.bfloat16).reshape(2 * FRAMES, POLS, BEAMS)
            return carry

        for n in range(W_CHUNKS):
            copies[n].wait()
            lax.fori_loop(W_STEP * n, W_STEP * (n + 1), one_channel, 0, unroll=3)


def finish(section, weights, received):
    vmem = pl.BlockSpec(memory_space=pltpu.VMEM)
    vis, beam = pl.pallas_call(
        finish_kernel,
        out_shape=(
            jax.ShapeDtypeStruct((VIS_LOCAL, INPUTS, INPUTS), jnp.bfloat16),
            jax.ShapeDtypeStruct((PER_GROUP, 2 * FRAMES, POLS, BEAMS), jnp.bfloat16),
        ),
        in_specs=[
            pl.BlockSpec(memory_space=pltpu.SMEM),
            pl.BlockSpec(memory_space=pl.ANY),
            vmem,
            vmem,
            vmem,
        ],
        out_specs=(vmem, vmem),
        scratch_shapes=[
            pltpu.VMEM((2, PER_GROUP * 24, 128), jnp.float32),
            pltpu.VMEM((5, INPUTS, 128), jnp.bfloat16),
            pltpu.VMEM((PER_GROUP, INPUTS, BEAMS), jnp.bfloat16),
            pltpu.SemaphoreType.DMA((W_CHUNKS,)),
        ],
        name="finish",
    )(
        section,
        weights,
        received,
        jnp.asarray(swap_table(), jnp.bfloat16),
        jnp.asarray(split_table(), jnp.bfloat16),
    )
    tied = beam.reshape(PER_GROUP, 2, FRAMES, POLS, BEAMS).transpose(0, 1, 3, 2, 4)
    return vis, tied


def split2(value):
    high = value.astype(jnp.bfloat16)
    return high, (value - high.astype(jnp.float32)).astype(jnp.bfloat16)


def split_const(table):
    table = np.asarray(table, np.float32)
    high = table.astype(jnp.bfloat16)
    return high, (table - high.astype(np.float32)).astype(jnp.bfloat16)


def taper_table():
    index = np.arange(TAPS * NCH, dtype=np.float64)
    offset = (index + 0.5 - TAPS * NCH / 2.0) / NCH
    window = 0.5 - 0.5 * np.cos(2.0 * np.pi * (index + 0.5) / (TAPS * NCH))
    table = (np.sinc(offset) * window).reshape(TAPS, PER_GROUP, 1, 128)
    table = np.broadcast_to(table, (TAPS, PER_GROUP, POLS, 128))
    return table.reshape(TAPS, 2 * PER_GROUP, 128).astype(np.float32)


def outer_table():
    angle = 2.0 * np.pi * (np.outer(np.arange(48), np.arange(48)) % 48) / 48.0
    cos, sin = np.cos(angle), np.sin(angle)
    table = np.zeros((POLS, 2, 48, 2, 48, POLS))
    for pol in range(POLS):
        table[pol, 0, :, 0, :, pol] = cos
        table[pol, 0, :, 1, :, pol] = sin
        table[pol, 1, :, 0, :, pol] = -sin
        table[pol, 1, :, 1, :, pol] = cos
    return table.reshape(192, 192)


def twist_tables():
    angle = 2.0 * np.pi * np.outer(np.arange(48), np.arange(128)) / NCH
    return np.stack([np.cos(angle), np.sin(angle)]).astype(np.float32)


def inner_table():
    angle = 2.0 * np.pi * (np.outer(np.arange(128), np.arange(128)) % 128) / 128.0
    return np.concatenate([np.cos(angle), np.sin(angle)], axis=1)


def spread_table():
    row, col = np.arange(384)[:, None], np.arange(640)[None, :]
    return ((row % 48 == col // 12) & (col < 576)).astype(np.float32)


def make_weights(delays, first, w_ref):
    delay = delays.astype(jnp.float32).T.astype(jnp.int32)
    turn = 2.0 * math.pi / PERIOD
    start = (delay * first & (PERIOD - 1)).astype(jnp.float32) * turn
    step = delay.astype(jnp.float32) * turn
    state = (jnp.cos(start), jnp.sin(start), jnp.cos(step), jnp.sin(step))
    for sb in range(8):
        cs, sn, dc, ds = (t[16 * sb : 16 * sb + 16] for t in state)

        def advance(k, carry):
            c, s = carry
            w_ref[k, 16 * sb : 16 * sb + 16, :] = c.astype(jnp.bfloat16)
            w_ref[k, 128 + 16 * sb : 128 + 16 * sb + 16, :] = s.astype(jnp.bfloat16)
            return (c * dc - s * ds, c * ds + s * dc)

        lax.fori_loop(0, PER_GROUP, advance, (cs, sn), unroll=4)


def channelize_kernel(
    flag_ref,
    volt_hbm,
    band_hbm,
    delays_hbm,
    taper_hbm,
    outer_h_hbm,
    outer_l_hbm,
    twist_hbm,
    inner_h_hbm,
    inner_l_hbm,
    spread_hbm,
    recv_ref,
    w_hbm,
    volt_ref,
    band_ref,
    delays_ref,
    taper_ref,
    outer_h_ref,
    outer_l_ref,
    twist_ref,
    inner_h_ref,
    inner_l_ref,
    spread_ref,
    fh_ref,
    fl_ref,
    y_ref,
    o_ref,
    send_ref,
    pow_ref,
    w_ref,
    load_sem,
    send_sem,
    recv_sem,
    own_sem,
    w_sem,
    ready_sem,
):
    me, sec = lax.axis_index("stn"), lax.axis_index("sec")
    plane, place = me // PLANE, lax.rem(me, PLANE)
    barrier = pltpu.get_barrier_semaphore()
    loads = [
        pltpu.make_async_copy(src, dst, load_sem.at[n])
        for n, (src, dst) in enumerate(
            (
                (volt_hbm, volt_ref),
                (taper_hbm, taper_ref),
                (band_hbm, band_ref),
                (spread_hbm, spread_ref),
                (outer_h_hbm, outer_h_ref),
                (outer_l_hbm, outer_l_ref),
                (twist_hbm, twist_ref),
                (inner_h_hbm, inner_h_ref),
                (inner_l_hbm, inner_l_ref),
                (delays_hbm, delays_ref),
            )
        )
    ]
    for load in loads:
        load.start()

    for i in range(1, PLANE):
        other = plane * PLANE + lax.rem(place + i, PLANE)
        pl.semaphore_signal(barrier, inc=1, device_id=(other, sec), device_id_type=MESH)
    for i in range(1, SECTIONS):
        other = lax.rem(sec + i, SECTIONS)
        pl.semaphore_signal(barrier, inc=1, device_id=(me, other), device_id_type=MESH)
    for load in loads[:-1]:
        load.wait()

    group = lax.broadcasted_iota(jnp.int32, (8, 128), 0)
    lane8 = lax.broadcasted_iota(jnp.int32, (8, 128), 1)
    spread_parts = []
    for q in range(3):
        inside = (lane8 + 128 * q >= 48 * group) & (lane8 + 128 * q < 48 * group + 48)
        tiles = [
            jnp.where(inside, band_ref[0:1, 384 * t + 128 * q : 384 * t + 128 * q + 128], 0.0)
            for t in range(16)
        ]
        spread_parts.append(jnp.concatenate(tiles, axis=0))
    band_h, band_l = split2(jnp.concatenate(spread_parts, axis=1))

    for part in range(2):
        for chunk in range(6):
            rows = slice(16 * chunk, 16 * chunk + 16)
            taps = [taper_ref[j, rows, :] for j in range(TAPS)]
            blocks = [
                volt_ref[part, 96 * n + 16 * chunk : 96 * n + 16 * chunk + 16, :].astype(jnp.float32)
                for n in range(FRAMES + TAPS - 1)
            ]
            for m in range(FRAMES):
                total = taps[0] * blocks[m]
                for j in range(1, TAPS):
                    total = total + taps[j] * blocks[m + j]
                high, low = split2(total)
                at = slice(96 * part + 16 * chunk, 96 * part + 16 * chunk + 16)
                fh_ref[at, 128 * m : 128 * m + 128] = high
                fl_ref[at, 128 * m : 128 * m + 128] = low

    cos, sin = twist_ref[0], twist_ref[1]
    for pair in range(FRAMES // 2):
        lanes = slice(256 * pair, 256 * pair + 256)
        fh = fh_ref[:, lanes]
        seg = dot_f32(outer_h_ref[...], fh, NN)
        seg = seg + dot_f32(outer_l_ref[...], fh, NN)
        seg = seg + dot_f32(outer_h_ref[...], fl_ref[:, lanes], NN)
        for half in range(2):
            m = 2 * pair + half
            for pol in range(POLS):
                sr = seg[96 * pol : 96 * pol + 48, 128 * half : 128 * half + 128]
                si = seg[96 * pol + 48 : 96 * pol + 96, 128 * half : 128 * half + 128]
                yr = sr * cos + si * sin
                yi = si * cos - sr * sin
                real_rows = pl.ds(m, 48, stride=12)
                imag_rows = pl.ds(FRAMES + m, 48, stride=12)
                y_ref[2 * pol, real_rows, :] = yr
                y_ref[2 * pol + 1, real_rows, :] = yi
                y_ref[2 * pol, imag_rows, :] = yi
                y_ref[2 * pol + 1, imag_rows, :] = -yr

    powers = [jnp.zeros((8, 128), jnp.float32) for _ in range(POLS)]
    for first, count in ((0, 2), (2, 2), (4, 1)):
        width = 128 * count
        depth = min(width, 576 - 128 * first)
        columns = spread_ref[:, 128 * first : 128 * first + width]
        spread = dot_f32(band_h, columns, NN) + dot_f32(band_l, columns, NN)
        for pol in range(POLS):
            y = jnp.concatenate(
                [y_ref[2 * pol + t, 128 * first : 128 * first + depth, :] for t in range(2)], axis=1
            )
            if depth < width:
                y = jnp.concatenate([y, jnp.zeros((width - depth, 256), jnp.float32)], axis=0)
            yh, yl = split2(y)
            out = dot_f32(inner_h_ref[...], yh, NT)
            out = out + dot_f32(inner_l_ref[...], yh, NT)
            out = out + dot_f32(inner_h_ref[...], yl, NT)
            out = out * spread
            square = out * out
            for t in range(count):
                piece = slice(128 * t, 128 * t + 128)
                o_ref[first + t, pl.ds(pol, 128, stride=2), :] = out[:, piece]
                powers[pol] = powers[pol] + jnp.sum(square[:, piece].reshape(16, 8, 128), axis=0)
    for j in range(4):
        send_ref[j] = o_ref[j].astype(jnp.bfloat16).reshape(128, 2, 128)
    lane = lax.broadcasted_iota(jnp.int32, (1, 128), 1)
    totals = [jnp.sum(p, keepdims=True) for p in powers]
    pow_ref[SECTIONS] = jnp.where(lane < 64, totals[0], totals[1])

    pl.semaphore_wait(barrier, PLANE - 1 + SECTIONS - 1 + plane)

    def greet_later(z, carry):
        pl.semaphore_signal(
            barrier, inc=1, device_id=(z * PLANE + place, sec), device_id_type=MESH
        )
        return carry

    def greet_earlier(z, carry):
        pl.semaphore_signal(
            ready_sem.at[plane], inc=1, device_id=(z * PLANE + place, sec), device_id_type=MESH
        )
        return carry

    lax.fori_loop(0, plane, greet_earlier, 0)
    lax.fori_loop(plane + 1, PLANES, greet_later, 0)

    def power_copy(j):
        return pltpu.make_async_remote_copy(
            src_ref=pow_ref.at[SECTIONS],
            dst_ref=pow_ref.at[sec],
            send_sem=send_sem.at[0],
            recv_sem=recv_sem.at[0],
            device_id=(me, lax.rem(sec + j, SECTIONS)),
            device_id_type=MESH,
        )

    for j in range(1, SECTIONS):
        power_copy(j).start()

    def block_copy(to, tiles):
        return pltpu.make_async_remote_copy(
            src_ref=send_ref.at[tiles, to],
            dst_ref=recv_ref.at[tiles, me],
            send_sem=send_sem.at[1],
            recv_sem=recv_sem.at[1],
            device_id=(to, sec),
            device_id_type=MESH,
        )

    body, tail, whole = pl.ds(0, 4), pl.ds(4, 1), pl.ds(0, 5)

    def send_plane(z, tiles, start):
        for i in range(start, PLANE):
            block_copy(z * PLANE + lax.rem(place + i, PLANE), tiles).start()

    def send_entered(tiles):
        def one(n, carry):
            odd = lax.rem(n, 2)
            z = (1 - odd) * (n // 2) + odd * (plane - 1 - n // 2)
            send_plane(z, tiles, 0)
            return carry

        send_plane(plane, tiles, 1)
        lax.fori_loop(0, plane, one, 0)

    send_entered(body)

    def bytes_of(ref, slot):
        return pltpu.make_async_remote_copy(
            src_ref=ref,
            dst_ref=ref,
            send_sem=send_sem.at[slot],
            recv_sem=recv_sem.at[slot],
            device_id=(me, sec),
            device_id_type=MESH,
        )

    three = bytes_of(pow_ref.at[pl.ds(0, SECTIONS - 1)], 0)
    three.wait_send()
    three.wait_recv()
    mine = lax.broadcasted_iota(jnp.int32, (1, 128), 1) * 0 + sec
    total = pow_ref[SECTIONS]
    for other in range(SECTIONS):
        total = total + jnp.where(mine == other, 0.0, pow_ref[other])
    mean = total * (1.0 / (SECTIONS * FRAMES * NCH))
    gain = jnp.where(flag_ref[0] == 1, 0.0, 1.0 / jnp.sqrt(mean + 1e-05))
    g0 = gain.astype(jnp.bfloat16).astype(jnp.float32)
    g1 = (gain - g0).astype(jnp.bfloat16).astype(jnp.float32)
    g2 = gain - g0 - g1
    row = lax.broadcasted_iota(jnp.int32, (8, 128), 0)
    col = lax.broadcasted_iota(jnp.int32, (8, 128), 1)
    patch = jnp.zeros((8, 128), jnp.float32)
    for at, g in ((0, g0), (1, g1), (2, g2)):
        pair = jnp.where(row % 2 == 0, g[:, 0:1], g[:, 64:65])
        patch = jnp.where(col == GAIN_LANE + at, pair, patch)
    patch = jnp.broadcast_to(patch[None], (INPUTS // 8, 8, 128)).reshape(INPUTS, 128)
    wide = lax.broadcasted_iota(jnp.int32, (INPUTS, 128), 1)
    tile = jnp.where(wide < GAIN_LANE, o_ref[4], patch)
    send_ref[4] = tile.astype(jnp.bfloat16).reshape(128, 2, 128)
    send_entered(tail)

    def send_later(z, carry):
        pl.semaphore_wait(ready_sem.at[z], 1)
        send_plane(z, whole, 0)
        return carry

    lax.fori_loop(plane + 1, PLANES, send_later, 0)
    own = pltpu.make_async_copy(send_ref.at[:, me], recv_ref.at[:, me], own_sem)
    own.start()
    loads[-1].wait()
    make_weights(delays_ref[...], sec * NCH + me * PER_GROUP, w_ref)
    save = pltpu.make_async_copy(w_ref, w_hbm, w_sem)
    save.start()
    own.wait()
    sent = bytes_of(send_ref.at[:, pl.ds(0, STATIONS - 1)], 1)
    sent.wait_send()
    save.wait()
    landed = bytes_of(recv_ref.at[:, pl.ds(0, STATIONS - 1)], 1)
    landed.wait_recv()


def channelize(flags, volts, band, delays):
    outer_h, outer_l = split_const(outer_table())
    inner_h, inner_l = split_const(inner_table())
    operands = [
        volts,
        band,
        delays,
        jnp.asarray(taper_table()),
        jnp.asarray(outer_h),
        jnp.asarray(outer_l),
        jnp.asarray(twist_tables()),
        jnp.asarray(inner_h),
        jnp.asarray(inner_l),
        jnp.asarray(spread_table(), jnp.bfloat16),
    ]
    anywhere = pl.BlockSpec(memory_space=pl.ANY)
    return pl.pallas_call(
        channelize_kernel,
        out_shape=(
            jax.ShapeDtypeStruct((5, STATIONS, POLS, 128), jnp.bfloat16),
            jax.ShapeDtypeStruct((PER_GROUP, INPUTS, BEAMS), jnp.bfloat16),
        ),
        in_specs=[pl.BlockSpec(memory_space=pltpu.SMEM)] + [anywhere] * len(operands),
        out_specs=(anywhere, anywhere),
        scratch_shapes=[pltpu.VMEM(x.shape, x.dtype) for x in operands]
        + [
            pltpu.VMEM((192, 768), jnp.bfloat16),
            pltpu.VMEM((192, 768), jnp.bfloat16),
            pltpu.VMEM((4, 576, 128), jnp.float32),
            pltpu.VMEM((5, 256, 128), jnp.float32),
            pltpu.VMEM((5, STATIONS, POLS, 128), jnp.bfloat16),
            pltpu.VMEM((5, 1, 128), jnp.float32),
            pltpu.VMEM((PER_GROUP, INPUTS, BEAMS), jnp.bfloat16),
            pltpu.SemaphoreType.DMA((len(operands),)),
            pltpu.SemaphoreType.DMA((2,)),
            pltpu.SemaphoreType.DMA((2,)),
            pltpu.SemaphoreType.DMA,
            pltpu.SemaphoreType.DMA,
            pltpu.SemaphoreType.REGULAR((PLANES,)),
        ],
        compiler_params=pltpu.CompilerParams(collective_id=0, has_side_effects=True),
        name="channelize",
    )(flags, *operands)


def per_device(voltages, bandpass, station_flags, delays, section):
    volts = voltages.reshape(2, POLS, 624, 128).transpose(0, 2, 1, 3).reshape(2, 1248, 128)
    turned, weights = channelize(station_flags, volts, bandpass, delays)
    vis, tied = finish(section, weights, turned.reshape(5, INPUTS, 128))
    return (vis[None], tied[None])


def solution(mesh):
    return jax.shard_map(
        per_device,
        mesh=mesh,
        in_specs=(P(None, "stn", "sec", None, None), P("sec", None), P("stn"), P(), P()),
        out_specs=(P("sec", "stn", None, None), P("sec", "stn", None, None, None, None)),
        check_vma=False,
    )
```

```python
import functools
import math

import jax
import jax.numpy as jnp
import numpy as np
from jax import lax
from jax.experimental import pallas as pl
from jax.experimental.pallas import tpu as pltpu
from jax.sharding import PartitionSpec as P

POLS = 2
NCH = 6144
TAPS = 8
FRAMES = 6
AVG = 12
BEAMS = 256
STATIONS = 128
INPUTS = STATIONS * POLS
PER_GROUP = 48
VIS_LOCAL = PER_GROUP // AVG
BLOCK = AVG * 2 * FRAMES
PERIOD = 65536
GAIN_LANE = 64
OUT_CHUNKS = 4
OUT_STEP = PER_GROUP // OUT_CHUNKS
PLANES = 8
PLANE = STATIONS // PLANES
SECTIONS = 4
MESH = pl.DeviceIdType.MESH

NT = (((1,), (1,)), ((), ()))
NN = (((1,), (0,)), ((), ()))


def dot_f32(lhs, rhs, dims):
    return lax.dot_general(lhs, rhs, dims, preferred_element_type=jnp.float32)


def swap_table():
    table = np.zeros((VIS_LOCAL, INPUTS, INPUTS), np.float32)
    for v in range(VIS_LOCAL):
        for q in range(BLOCK):
            real = q % 12 < 6
            table[v, 16 * v + q, 16 * v + (q + 6 if real else q - 6)] = -1.0 if real else 1.0
    return table


def split_table():
    table = np.zeros((INPUTS, INPUTS), np.float32)
    for pol in range(POLS):
        for station in range(STATIONS):
            table[pol * STATIONS + station, station * POLS + pol] = 1.0
    return table


def finish_kernel(
    section_ref,
    w_ref,
    r_ref,
    swap_ref,
    split_ref,
    vis_hbm,
    beam_hbm,
    vis_ref,
    beam_ref,
    xl_ref,
    xs_ref,
    out_sem,
    zero_sem,
):
    is_beam = jnp.max(section_ref[...]) == 1.0

    @pl.when(jnp.logical_not(is_beam))
    def _():
        beam_ref[...] = jnp.zeros_like(beam_ref)
        zero = pltpu.make_async_copy(beam_ref, beam_hbm, zero_sem)
        zero.start()
        copies = []
        last = r_ref[VIS_LOCAL]
        gain_col = jnp.sum(
            last[:, GAIN_LANE : GAIN_LANE + 3].astype(jnp.float32), axis=1, keepdims=True
        )
        gain_col = gain_col * (1.0 / math.sqrt(FRAMES * AVG))
        lane8 = lax.broadcasted_iota(jnp.int32, (8, 128), 1)
        pick = jnp.where((lane8 >= GAIN_LANE) & (lane8 < GAIN_LANE + 3), 1.0, 0.0)
        gain_row = dot_f32(pick.astype(jnp.bfloat16), last, NT)[0:1, :]
        rows = lax.broadcasted_iota(jnp.int32, (INPUTS, INPUTS), 0)
        cols = lax.broadcasted_iota(jnp.int32, (INPUTS, INPUTS), 1)
        for v in range(VIS_LOCAL):
            left = jnp.concatenate([r_ref[v], r_ref[v + 1]], axis=1)
            inside = (cols >= 16 * v) & (cols < 16 * v + BLOCK)
            same = jnp.where(inside, left.astype(jnp.float32), 0.0).astype(jnp.bfloat16)
            other = dot_f32(left, swap_ref[v], NT).astype(jnp.bfloat16)
            real = dot_f32(left, same, NT)
            imag = dot_f32(left, other, NT)
            packed = jnp.where(rows <= cols, real, imag)
            vis_ref[v] = (packed * gain_col * gain_row).astype(jnp.bfloat16)
            copies.append(pltpu.make_async_copy(vis_ref.at[v], vis_hbm.at[v], out_sem.at[v]))
            copies[v].start()
        for copy in copies:
            copy.wait()
        zero.wait()

    @pl.when(is_beam)
    def _():
        vis_ref[...] = jnp.zeros_like(vis_ref)
        zero = pltpu.make_async_copy(vis_ref, vis_hbm, zero_sem)
        zero.start()
        gain = None
        for j in range(VIS_LOCAL, -1, -1):
            part = dot_f32(split_ref[...], r_ref[j], NN)
            if gain is None:
                gain = jnp.sum(part[:, GAIN_LANE : GAIN_LANE + 3], axis=1, keepdims=True)
            xs_ref[j] = (part * gain).astype(jnp.bfloat16)
        q_row = lax.broadcasted_iota(jnp.int32, (BLOCK, INPUTS), 0)
        q_col = lax.broadcasted_iota(jnp.int32, (BLOCK, INPUTS), 1)
        for v in range(VIS_LOCAL):
            window = jnp.concatenate([xs_ref[v], xs_ref[v + 1]], axis=1)
            keep = jnp.where(q_col == q_row + 16 * v, 1.0, 0.0).astype(jnp.bfloat16)
            plain = dot_f32(keep, window, NT)
            other = dot_f32(swap_ref[v, 16 * v : 16 * v + BLOCK, :], window, NT)
            for pol in range(POLS):
                rows = pl.ds(2 * BLOCK * v + pol, BLOCK, stride=2)
                half = slice(128 * pol, 128 * pol + 128)
                xl_ref[0, rows, :] = plain[:, half]
                xl_ref[1, rows, :] = other[:, half]
        scale = 1.0 / math.sqrt(STATIONS)

        def one_channel(k, carry):
            rows = pl.ds(pl.multiple_of(24 * k, 8), 24)
            left = jnp.concatenate([xl_ref[0, rows, :], xl_ref[1, rows, :]], axis=1)
            out = dot_f32(left.astype(jnp.bfloat16), w_ref[k], NN) * scale
            beam_ref[k] = out.astype(jnp.bfloat16).reshape(2 * FRAMES, POLS, BEAMS)
            return carry

        copies = []
        for n in range(OUT_CHUNKS):
            lax.fori_loop(OUT_STEP * n, OUT_STEP * (n + 1), one_channel, 0, unroll=4)
            part = pl.ds(OUT_STEP * n, OUT_STEP)
            copies.append(
                pltpu.make_async_copy(beam_ref.at[part], beam_hbm.at[part], out_sem.at[n])
            )
            copies[n].start()
        for copy in copies:
            copy.wait()
        zero.wait()


def finish(section, weights, received, swap, split):
    vmem = pl.BlockSpec(memory_space=pltpu.VMEM)
    anywhere = pl.BlockSpec(memory_space=pl.ANY)
    vis_shape = (VIS_LOCAL, INPUTS, INPUTS)
    beam_shape = (PER_GROUP, 2 * FRAMES, POLS, BEAMS)
    vis, beam = pl.pallas_call(
        finish_kernel,
        out_shape=(
            jax.ShapeDtypeStruct(vis_shape, jnp.bfloat16),
            jax.ShapeDtypeStruct(beam_shape, jnp.bfloat16),
        ),
        in_specs=[vmem] * 5,
        out_specs=(anywhere, anywhere),
        scratch_shapes=[
            pltpu.VMEM(vis_shape, jnp.bfloat16),
            pltpu.VMEM(beam_shape, jnp.bfloat16),
            pltpu.VMEM((2, PER_GROUP * 24, 128), jnp.float32),
            pltpu.VMEM((5, INPUTS, 128), jnp.bfloat16),
            pltpu.SemaphoreType.DMA((4,)),
            pltpu.SemaphoreType.DMA,
        ],
        compiler_params=pltpu.CompilerParams(vmem_limit_bytes=24 << 20),
        name="finish",
    )(section, weights, received, swap, split)
    tied = beam.reshape(PER_GROUP, 2, FRAMES, POLS, BEAMS).transpose(0, 1, 3, 2, 4)
    return vis, tied


def split2(value):
    high = value.astype(jnp.bfloat16)
    return high, (value - high.astype(jnp.float32)).astype(jnp.bfloat16)


def split_const(table):
    table = np.asarray(table, np.float32)
    high = table.astype(jnp.bfloat16)
    return high, (table - high.astype(np.float32)).astype(jnp.bfloat16)


def taper_table():
    index = np.arange(TAPS * NCH, dtype=np.float64)
    offset = (index + 0.5 - TAPS * NCH / 2.0) / NCH
    window = 0.5 - 0.5 * np.cos(2.0 * np.pi * (index + 0.5) / (TAPS * NCH))
    table = (np.sinc(offset) * window).reshape(TAPS, PER_GROUP, 1, 128)
    table = np.broadcast_to(table, (TAPS, PER_GROUP, POLS, 128))
    return table.reshape(TAPS, 2 * PER_GROUP, 128).astype(np.float32)


def outer_table():
    angle = 2.0 * np.pi * (np.outer(np.arange(48), np.arange(48)) % 48) / 48.0
    cos, sin = np.cos(angle), np.sin(angle)
    table = np.zeros((POLS, 2, 48, 2, 48, POLS))
    for pol in range(POLS):
        table[pol, 0, :, 0, :, pol] = cos
        table[pol, 0, :, 1, :, pol] = sin
        table[pol, 1, :, 0, :, pol] = -sin
        table[pol, 1, :, 1, :, pol] = cos
    return table.reshape(192, 192)


def twist_tables():
    angle = 2.0 * np.pi * np.outer(np.arange(48), np.arange(128)) / NCH
    return np.stack([np.cos(angle), np.sin(angle)]).astype(np.float32)


def inner_table():
    angle = 2.0 * np.pi * (np.outer(np.arange(128), np.arange(128)) % 128) / 128.0
    return np.concatenate([np.cos(angle), np.sin(angle)], axis=1)


def spread_table():
    row, col = np.arange(384)[:, None], np.arange(640)[None, :]
    return ((row % 48 == col // 12) & (col < 576)).astype(np.float32)


def make_weights(delays, first, w_ref):
    delay = delays.astype(jnp.float32).T.astype(jnp.int32)
    turn = 2.0 * math.pi / PERIOD
    start = (delay * first & (PERIOD - 1)).astype(jnp.float32) * turn
    step = delay.astype(jnp.float32) * turn
    state = (jnp.cos(start), jnp.sin(start), jnp.cos(step), jnp.sin(step))
    for sb in range(8):
        cs, sn, dc, ds = (t[16 * sb : 16 * sb + 16] for t in state)

        def advance(k, carry):
            c, s = carry
            w_ref[k, 16 * sb : 16 * sb + 16, :] = c.astype(jnp.bfloat16)
            w_ref[k, 128 + 16 * sb : 128 + 16 * sb + 16, :] = s.astype(jnp.bfloat16)
            return (c * dc - s * ds, c * ds + s * dc)

        lax.fori_loop(0, PER_GROUP, advance, (cs, sn), unroll=4)


def channelize_kernel(
    flag_ref,
    volt_hbm,
    band_hbm,
    delays_hbm,
    taper_hbm,
    outer_h_hbm,
    outer_l_hbm,
    twist_hbm,
    inner_h_hbm,
    inner_l_hbm,
    spread_hbm,
    section_hbm,
    swap_hbm,
    split_hbm,
    recv_ref,
    w_ref,
    section_ref,
    swap_ref,
    split_ref,
    volt_ref,
    band_ref,
    delays_ref,
    taper_ref,
    outer_h_ref,
    outer_l_ref,
    twist_ref,
    inner_h_ref,
    inner_l_ref,
    spread_ref,
    choice_ref,
    fh_ref,
    fl_ref,
    y_ref,
    o_ref,
    send_ref,
    pow_ref,
    load_sem,
    send_sem,
    recv_sem,
    own_sem,
    ready_sem,
):
    me, sec = lax.axis_index("stn"), lax.axis_index("sec")
    plane, place = me // PLANE, lax.rem(me, PLANE)
    barrier = pltpu.get_barrier_semaphore()
    loads = [
        pltpu.make_async_copy(src, dst, load_sem.at[n])
        for n, (src, dst) in enumerate(
            (
                (volt_hbm, volt_ref),
                (taper_hbm, taper_ref),
                (band_hbm, band_ref),
                (spread_hbm, spread_ref),
                (outer_h_hbm, outer_h_ref),
                (outer_l_hbm, outer_l_ref),
                (twist_hbm, twist_ref),
                (inner_h_hbm, inner_h_ref),
                (inner_l_hbm, inner_l_ref),
                (delays_hbm, delays_ref),
                (section_hbm, choice_ref),
                (swap_hbm, swap_ref),
                (split_hbm, split_ref),
            )
        )
    ]
    for load in loads:
        load.start()

    for i in range(1, PLANE):
        other = plane * PLANE + lax.rem(place + i, PLANE)
        pl.semaphore_signal(barrier, inc=1, device_id=(other, sec), device_id_type=MESH)
    for i in range(1, SECTIONS):
        other = lax.rem(sec + i, SECTIONS)
        pl.semaphore_signal(barrier, inc=1, device_id=(me, other), device_id_type=MESH)
    def greet_later(z, carry):
        pl.semaphore_signal(
            barrier, inc=1, device_id=(z * PLANE + place, sec), device_id_type=MESH
        )
        return carry

    def greet_earlier(z, carry):
        pl.semaphore_signal(
            ready_sem.at[plane], inc=1, device_id=(z * PLANE + place, sec), device_id_type=MESH
        )
        return carry

    def meet():
        pl.semaphore_wait(barrier, PLANE - 1 + SECTIONS - 1 + plane)
        lax.fori_loop(0, plane, greet_earlier, 0)
        lax.fori_loop(plane + 1, PLANES, greet_later, 0)

    late = (place // 2 == 4) | (place // 2 == 5)

    @pl.when(late)
    def _():
        meet()

    for load in loads[:9]:
        load.wait()

    group = lax.broadcasted_iota(jnp.int32, (8, 128), 0)
    lane8 = lax.broadcasted_iota(jnp.int32, (8, 128), 1)
    spread_parts = []
    for q in range(3):
        inside = (lane8 + 128 * q >= 48 * group) & (lane8 + 128 * q < 48 * group + 48)
        tiles = [
            jnp.where(inside, band_ref[0:1, 384 * t + 128 * q : 384 * t + 128 * q + 128], 0.0)
            for t in range(16)
        ]
        spread_parts.append(jnp.concatenate(tiles, axis=0))
    band_h, band_l = split2(jnp.concatenate(spread_parts, axis=1))

    for part in range(2):
        for chunk in range(6):
            rows = slice(16 * chunk, 16 * chunk + 16)
            taps = [taper_ref[j, rows, :] for j in range(TAPS)]
            blocks = [
                volt_ref[part, 96 * n + 16 * chunk : 96 * n + 16 * chunk + 16, :].astype(jnp.float32)
                for n in range(FRAMES + TAPS - 1)
            ]
            for m in range(FRAMES):
                total = taps[0] * blocks[m]
                for j in range(1, TAPS):
                    total = total + taps[j] * blocks[m + j]
                high, low = split2(total)
                at = slice(96 * part + 16 * chunk, 96 * part + 16 * chunk + 16)
                fh_ref[at, 128 * m : 128 * m + 128] = high
                fl_ref[at, 128 * m : 128 * m + 128] = low

    cos, sin = twist_ref[0], twist_ref[1]
    for pair in range(FRAMES // 2):
        lanes = slice(256 * pair, 256 * pair + 256)
        fh = fh_ref[:, lanes]
        seg = dot_f32(outer_h_ref[...], fh, NN)
        seg = seg + dot_f32(outer_l_ref[...], fh, NN)
        seg = seg + dot_f32(outer_h_ref[...], fl_ref[:, lanes], NN)
        for half in range(2):
            m = 2 * pair + half
            for pol in range(POLS):
                sr = seg[96 * pol : 96 * pol + 48, 128 * half : 128 * half + 128]
                si = seg[96 * pol + 48 : 96 * pol + 96, 128 * half : 128 * half + 128]
                yr = sr * cos + si * sin
                yi = si * cos - sr * sin
                real_rows = pl.ds(m, 48, stride=12)
                imag_rows = pl.ds(FRAMES + m, 48, stride=12)
                y_ref[2 * pol, real_rows, :] = yr
                y_ref[2 * pol + 1, real_rows, :] = yi
                y_ref[2 * pol, imag_rows, :] = yi
                y_ref[2 * pol + 1, imag_rows, :] = -yr

    powers = [jnp.zeros((8, 128), jnp.float32) for _ in range(POLS)]
    for first, count in ((0, 2), (2, 2), (4, 1)):
        width = 128 * count
        depth = min(width, 576 - 128 * first)
        columns = spread_ref[:, 128 * first : 128 * first + width]
        spread = dot_f32(band_h, columns, NN) + dot_f32(band_l, columns, NN)
        for pol in range(POLS):
            y = jnp.concatenate(
                [y_ref[2 * pol + t, 128 * first : 128 * first + depth, :] for t in range(2)], axis=1
            )
            if depth < width:
                y = jnp.concatenate([y, jnp.zeros((width - depth, 256), jnp.float32)], axis=0)
            yh, yl = split2(y)
            out = dot_f32(inner_h_ref[...], yh, NT)
            out = out + dot_f32(inner_l_ref[...], yh, NT)
            out = out + dot_f32(inner_h_ref[...], yl, NT)
            out = out * spread
            square = out * out
            for t in range(count):
                piece = slice(128 * t, 128 * t + 128)
                o_ref[first + t, pl.ds(pol, 128, stride=2), :] = out[:, piece]
                powers[pol] = powers[pol] + jnp.sum(square[:, piece].reshape(16, 8, 128), axis=0)
    for j in range(4):
        send_ref[j] = o_ref[j].astype(jnp.bfloat16).reshape(128, 2, 128)
    lane = lax.broadcasted_iota(jnp.int32, (1, 128), 1)
    totals = [jnp.sum(p, keepdims=True) for p in powers]
    pow_ref[SECTIONS] = jnp.where(lane < 64, totals[0], totals[1])

    @pl.when(jnp.logical_not(late))
    def _():
        meet()

    def power_copy(j):
        return pltpu.make_async_remote_copy(
            src_ref=pow_ref.at[SECTIONS],
            dst_ref=pow_ref.at[sec],
            send_sem=send_sem.at[0],
            recv_sem=recv_sem.at[0],
            device_id=(me, lax.rem(sec + j, SECTIONS)),
            device_id_type=MESH,
        )

    for j in range(1, SECTIONS):
        power_copy(j).start()

    def block_copy(to, tiles):
        return pltpu.make_async_remote_copy(
            src_ref=send_ref.at[tiles, to],
            dst_ref=recv_ref.at[tiles, me],
            send_sem=send_sem.at[1],
            recv_sem=recv_sem.at[1],
            device_id=(to, sec),
            device_id_type=MESH,
        )

    body, tail, whole = pl.ds(0, 4), pl.ds(4, 1), pl.ds(0, 5)

    def send_plane(z, tiles, start):
        for i in range(start, PLANE):
            block_copy(z * PLANE + lax.rem(place + i, PLANE), tiles).start()

    high = plane // 4
    near = plane * (1 - high) + 4 * high

    def send_entered(tiles):
        def first(n, carry):
            odd = lax.rem(n, 2)
            send_plane((1 - odd) * (n // 2) + odd * (near - 1 - n // 2), tiles, 0)
            return carry

        def then(z, carry):
            send_plane(z, tiles, 0)
            return carry

        lax.fori_loop(0, near, first, 0)
        lax.fori_loop(near, plane, then, 0)
        send_plane(plane, tiles, 1)

    send_entered(body)

    def bytes_of(ref, slot):
        return pltpu.make_async_remote_copy(
            src_ref=ref,
            dst_ref=ref,
            send_sem=send_sem.at[slot],
            recv_sem=recv_sem.at[slot],
            device_id=(me, sec),
            device_id_type=MESH,
        )

    three = bytes_of(pow_ref.at[pl.ds(0, SECTIONS - 1)], 0)
    three.wait_send()
    three.wait_recv()
    mine = lax.broadcasted_iota(jnp.int32, (1, 128), 1) * 0 + sec
    total = pow_ref[SECTIONS]
    for other in range(SECTIONS):
        total = total + jnp.where(mine == other, 0.0, pow_ref[other])
    mean = total * (1.0 / (SECTIONS * FRAMES * NCH))
    gain = jnp.where(flag_ref[0] == 1, 0.0, 1.0 / jnp.sqrt(mean + 1e-05))
    g0 = gain.astype(jnp.bfloat16).astype(jnp.float32)
    g1 = (gain - g0).astype(jnp.bfloat16).astype(jnp.float32)
    g2 = gain - g0 - g1
    row = lax.broadcasted_iota(jnp.int32, (8, 128), 0)
    col = lax.broadcasted_iota(jnp.int32, (8, 128), 1)
    patch = jnp.zeros((8, 128), jnp.float32)
    for at, g in ((0, g0), (1, g1), (2, g2)):
        pair = jnp.where(row % 2 == 0, g[:, 0:1], g[:, 64:65])
        patch = jnp.where(col == GAIN_LANE + at, pair, patch)
    patch = jnp.broadcast_to(patch[None], (INPUTS // 8, 8, 128)).reshape(INPUTS, 128)
    wide = lax.broadcasted_iota(jnp.int32, (INPUTS, 128), 1)
    tile = jnp.where(wide < GAIN_LANE, o_ref[4], patch)
    send_ref[4] = tile.astype(jnp.bfloat16).reshape(128, 2, 128)
    send_entered(tail)

    def send_later(z, carry):
        pl.semaphore_wait(ready_sem.at[z], 1)
        send_plane(z, whole, 0)
        return carry

    lax.fori_loop(plane + 1, PLANES, send_later, 0)
    own = pltpu.make_async_copy(send_ref.at[:, me], recv_ref.at[:, me], own_sem)
    own.start()
    for load in loads[10:]:
        load.wait()
    section_ref[...] = jnp.full((8, 128), choice_ref[sec]).astype(jnp.float32)
    loads[9].wait()
    make_weights(delays_ref[...], sec * NCH + me * PER_GROUP, w_ref)
    own.wait()
    sent = bytes_of(send_ref.at[:, pl.ds(0, STATIONS - 1)], 1)
    sent.wait_send()
    landed = bytes_of(recv_ref.at[:, pl.ds(0, STATIONS - 1)], 1)
    landed.wait_recv()


def channelize(volts, band, delays, flags, section):
    outer_h, outer_l = split_const(outer_table())
    inner_h, inner_l = split_const(inner_table())
    inputs = [
        volts,
        band,
        delays,
        jnp.asarray(taper_table()),
        jnp.asarray(outer_h),
        jnp.asarray(outer_l),
        jnp.asarray(twist_tables()),
        jnp.asarray(inner_h),
        jnp.asarray(inner_l),
        jnp.asarray(spread_table(), jnp.bfloat16),
    ]
    swap = jnp.asarray(swap_table(), jnp.bfloat16)
    split = jnp.asarray(split_table(), jnp.bfloat16)
    operands = [
        pltpu.with_memory_space_constraint(x, pltpu.HBM)
        for x in inputs + [section, swap, split]
    ]
    vmem = pl.BlockSpec(memory_space=pltpu.VMEM)
    return pl.pallas_call(
        channelize_kernel,
        out_shape=(
            pltpu.VMEM((5, STATIONS, POLS, 128), jnp.bfloat16),
            pltpu.VMEM((PER_GROUP, INPUTS, BEAMS), jnp.bfloat16),
            pltpu.VMEM((8, 128), jnp.float32),
            pltpu.VMEM(swap.shape, swap.dtype),
            pltpu.VMEM(split.shape, split.dtype),
        ),
        in_specs=[pl.BlockSpec(memory_space=pltpu.SMEM)]
        + [pl.BlockSpec(memory_space=pltpu.HBM)] * len(operands),
        out_specs=(vmem,) * 5,
        scratch_shapes=[pltpu.VMEM(x.shape, x.dtype) for x in inputs]
        + [
            pltpu.SMEM(section.shape, section.dtype),
            pltpu.VMEM((192, 768), jnp.bfloat16),
            pltpu.VMEM((192, 768), jnp.bfloat16),
            pltpu.VMEM((4, 576, 128), jnp.float32),
            pltpu.VMEM((5, 256, 128), jnp.float32),
            pltpu.VMEM((5, STATIONS, POLS, 128), jnp.bfloat16),
            pltpu.VMEM((5, 1, 128), jnp.float32),
            pltpu.SemaphoreType.DMA((len(operands),)),
            pltpu.SemaphoreType.DMA((2,)),
            pltpu.SemaphoreType.DMA((2,)),
            pltpu.SemaphoreType.DMA,
            pltpu.SemaphoreType.REGULAR((PLANES,)),
        ],
        compiler_params=pltpu.CompilerParams(
            collective_id=0, has_side_effects=True, vmem_limit_bytes=24 << 20
        ),
        name="channelize",
    )(flags, *operands)


def per_device(voltages, bandpass, station_flags, delays, section):
    volts = voltages.reshape(2, POLS, 624, 128).transpose(0, 2, 1, 3).reshape(2, 1248, 128)
    turned, weights, choice, swap, split = channelize(
        volts, bandpass, delays, station_flags, section
    )
    vis, tied = finish(choice, weights, turned.reshape(5, INPUTS, 128), swap, split)
    return (vis[None], tied[None])


def solution(mesh):
    return jax.shard_map(
        per_device,
        mesh=mesh,
        in_specs=(P(None, "stn", "sec", None, None), P("sec", None), P("stn"), P(), P()),
        out_specs=(P("sec", "stn", None, None), P("sec", "stn", None, None, None, None)),
        check_vma=False,
    )
```

```python
import functools
import math

import jax
import jax.numpy as jnp
import numpy as np
from jax import lax
from jax.experimental import pallas as pl
from jax.experimental.pallas import tpu as pltpu
from jax.sharding import PartitionSpec as P

POLS = 2
NCH = 6144
TAPS = 8
FRAMES = 6
AVG = 12
BEAMS = 256
STATIONS = 128
INPUTS = STATIONS * POLS
PER_GROUP = 48
VIS_LOCAL = PER_GROUP // AVG
BLOCK = AVG * 2 * FRAMES
PERIOD = 65536
GAIN_LANE = 64
OUT_CHUNKS = 4
OUT_STEP = PER_GROUP // OUT_CHUNKS
PLANES = 8
PLANE = STATIONS // PLANES
SECTIONS = 4
HALF = PLANES // 2
PLACES = (8, 9, 6, 7, 10, 11, 4, 5, 12, 13, 2, 3, 14, 15, 1, 0)
MESH = pl.DeviceIdType.MESH

NT = (((1,), (1,)), ((), ()))
NN = (((1,), (0,)), ((), ()))


def dot_f32(lhs, rhs, dims):
    return lax.dot_general(lhs, rhs, dims, preferred_element_type=jnp.float32)


def swap_table():
    table = np.zeros((VIS_LOCAL, INPUTS, INPUTS), np.float32)
    for v in range(VIS_LOCAL):
        for q in range(BLOCK):
            real = q % 12 < 6
            table[v, 16 * v + q, 16 * v + (q + 6 if real else q - 6)] = -1.0 if real else 1.0
    return table


def split_table():
    table = np.zeros((INPUTS, INPUTS), np.float32)
    for pol in range(POLS):
        for station in range(STATIONS):
            table[pol * STATIONS + station, station * POLS + pol] = 1.0
    return table


def finish_kernel(
    section_ref,
    w_ref,
    r_ref,
    swap_ref,
    split_ref,
    vis_hbm,
    beam_hbm,
    vis_ref,
    beam_ref,
    xl_ref,
    xs_ref,
    out_sem,
    zero_sem,
):
    is_beam = jnp.max(section_ref[...]) == 1.0

    @pl.when(jnp.logical_not(is_beam))
    def _():
        beam_ref[...] = jnp.zeros_like(beam_ref)
        zero = pltpu.make_async_copy(beam_ref, beam_hbm, zero_sem)
        zero.start()
        copies = []
        last = r_ref[VIS_LOCAL]
        gain_col = jnp.sum(
            last[:, GAIN_LANE : GAIN_LANE + 3].astype(jnp.float32), axis=1, keepdims=True
        )
        gain_col = gain_col * (1.0 / math.sqrt(FRAMES * AVG))
        lane8 = lax.broadcasted_iota(jnp.int32, (8, 128), 1)
        pick = jnp.where((lane8 >= GAIN_LANE) & (lane8 < GAIN_LANE + 3), 1.0, 0.0)
        gain_row = dot_f32(pick.astype(jnp.bfloat16), last, NT)[0:1, :]
        rows = lax.broadcasted_iota(jnp.int32, (INPUTS, INPUTS), 0)
        cols = lax.broadcasted_iota(jnp.int32, (INPUTS, INPUTS), 1)
        for v in range(VIS_LOCAL):
            left = jnp.concatenate([r_ref[v], r_ref[v + 1]], axis=1)
            inside = (cols >= 16 * v) & (cols < 16 * v + BLOCK)
            same = jnp.where(inside, left.astype(jnp.float32), 0.0).astype(jnp.bfloat16)
            other = dot_f32(left, swap_ref[v], NT).astype(jnp.bfloat16)
            real = dot_f32(left, same, NT)
            imag = dot_f32(left, other, NT)
            packed = jnp.where(rows <= cols, real, imag)
            vis_ref[v] = (packed * gain_col * gain_row).astype(jnp.bfloat16)
            copies.append(pltpu.make_async_copy(vis_ref.at[v], vis_hbm.at[v], out_sem.at[v]))
            copies[v].start()
        for copy in copies:
            copy.wait()
        zero.wait()

    @pl.when(is_beam)
    def _():
        vis_ref[...] = jnp.zeros_like(vis_ref)
        zero = pltpu.make_async_copy(vis_ref, vis_hbm, zero_sem)
        zero.start()
        gain = None
        for j in range(VIS_LOCAL, -1, -1):
            part = dot_f32(split_ref[...], r_ref[j], NN)
            if gain is None:
                gain = jnp.sum(part[:, GAIN_LANE : GAIN_LANE + 3], axis=1, keepdims=True)
            xs_ref[j] = (part * gain).astype(jnp.bfloat16)
        q_row = lax.broadcasted_iota(jnp.int32, (BLOCK, INPUTS), 0)
        q_col = lax.broadcasted_iota(jnp.int32, (BLOCK, INPUTS), 1)
        for v in range(VIS_LOCAL):
            window = jnp.concatenate([xs_ref[v], xs_ref[v + 1]], axis=1)
            keep = jnp.where(q_col == q_row + 16 * v, 1.0, 0.0).astype(jnp.bfloat16)
            plain = dot_f32(keep, window, NT)
            other = dot_f32(swap_ref[v, 16 * v : 16 * v + BLOCK, :], window, NT)
            for pol in range(POLS):
                rows = pl.ds(2 * BLOCK * v + pol, BLOCK, stride=2)
                half = slice(128 * pol, 128 * pol + 128)
                xl_ref[0, rows, :] = plain[:, half]
                xl_ref[1, rows, :] = other[:, half]
        scale = 1.0 / math.sqrt(STATIONS)

        def one_channel(k, carry):
            rows = pl.ds(pl.multiple_of(24 * k, 8), 24)
            left = jnp.concatenate([xl_ref[0, rows, :], xl_ref[1, rows, :]], axis=1)
            out = dot_f32(left.astype(jnp.bfloat16), w_ref[k], NN) * scale
            beam_ref[k] = out.astype(jnp.bfloat16).reshape(2 * FRAMES, POLS, BEAMS)
            return carry

        copies = []
        for n in range(OUT_CHUNKS):
            lax.fori_loop(OUT_STEP * n, OUT_STEP * (n + 1), one_channel, 0, unroll=4)
            part = pl.ds(OUT_STEP * n, OUT_STEP)
            copies.append(
                pltpu.make_async_copy(beam_ref.at[part], beam_hbm.at[part], out_sem.at[n])
            )
            copies[n].start()
        for copy in copies:
            copy.wait()
        zero.wait()


def finish(section, weights, received, swap, split):
    vmem = pl.BlockSpec(memory_space=pltpu.VMEM)
    anywhere = pl.BlockSpec(memory_space=pl.ANY)
    vis_shape = (VIS_LOCAL, INPUTS, INPUTS)
    beam_shape = (PER_GROUP, 2 * FRAMES, POLS, BEAMS)
    vis, beam = pl.pallas_call(
        finish_kernel,
        out_shape=(
            jax.ShapeDtypeStruct(vis_shape, jnp.bfloat16),
            jax.ShapeDtypeStruct(beam_shape, jnp.bfloat16),
        ),
        in_specs=[vmem] * 5,
        out_specs=(anywhere, anywhere),
        scratch_shapes=[
            pltpu.VMEM(vis_shape, jnp.bfloat16),
            pltpu.VMEM(beam_shape, jnp.bfloat16),
            pltpu.VMEM((2, PER_GROUP * 24, 128), jnp.float32),
            pltpu.VMEM((5, INPUTS, 128), jnp.bfloat16),
            pltpu.SemaphoreType.DMA((4,)),
            pltpu.SemaphoreType.DMA,
        ],
        compiler_params=pltpu.CompilerParams(vmem_limit_bytes=24 << 20),
        name="finish",
    )(section, weights, received, swap, split)
    tied = beam.reshape(PER_GROUP, 2, FRAMES, POLS, BEAMS).transpose(0, 1, 3, 2, 4)
    return vis, tied


def split2(value):
    high = value.astype(jnp.bfloat16)
    return high, (value - high.astype(jnp.float32)).astype(jnp.bfloat16)


def split_const(table):
    table = np.asarray(table, np.float32)
    high = table.astype(jnp.bfloat16)
    return high, (table - high.astype(np.float32)).astype(jnp.bfloat16)


def taper_table():
    index = np.arange(TAPS * NCH, dtype=np.float64)
    offset = (index + 0.5 - TAPS * NCH / 2.0) / NCH
    window = 0.5 - 0.5 * np.cos(2.0 * np.pi * (index + 0.5) / (TAPS * NCH))
    table = (np.sinc(offset) * window).reshape(TAPS, PER_GROUP, 1, 128)
    table = np.broadcast_to(table, (TAPS, PER_GROUP, POLS, 128))
    return table.reshape(TAPS, 2 * PER_GROUP, 128).astype(np.float32)


def outer_table():
    angle = 2.0 * np.pi * (np.outer(np.arange(48), np.arange(48)) % 48) / 48.0
    cos, sin = np.cos(angle), np.sin(angle)
    table = np.zeros((POLS, 2, 48, 2, 48, POLS))
    for pol in range(POLS):
        table[pol, 0, :, 0, :, pol] = cos
        table[pol, 0, :, 1, :, pol] = sin
        table[pol, 1, :, 0, :, pol] = -sin
        table[pol, 1, :, 1, :, pol] = cos
    return table.reshape(192, 192)


def twist_tables():
    angle = 2.0 * np.pi * np.outer(np.arange(48), np.arange(128)) / NCH
    return np.stack([np.cos(angle), np.sin(angle)]).astype(np.float32)


def inner_table():
    angle = 2.0 * np.pi * (np.outer(np.arange(128), np.arange(128)) % 128) / 128.0
    return np.concatenate([np.cos(angle), np.sin(angle)], axis=1)


def spread_table():
    row, col = np.arange(384)[:, None], np.arange(640)[None, :]
    return ((row % 48 == col // 12) & (col < 576)).astype(np.float32)


def make_weights(delays, first, w_ref):
    delay = delays.astype(jnp.float32).T.astype(jnp.int32)
    turn = 2.0 * math.pi / PERIOD
    start = (delay * first & (PERIOD - 1)).astype(jnp.float32) * turn
    step = delay.astype(jnp.float32) * turn
    state = (jnp.cos(start), jnp.sin(start), jnp.cos(step), jnp.sin(step))
    for sb in range(8):
        cs, sn, dc, ds = (t[16 * sb : 16 * sb + 16] for t in state)

        def advance(k, carry):
            c, s = carry
            w_ref[k, 16 * sb : 16 * sb + 16, :] = c.astype(jnp.bfloat16)
            w_ref[k, 128 + 16 * sb : 128 + 16 * sb + 16, :] = s.astype(jnp.bfloat16)
            return (c * dc - s * ds, c * ds + s * dc)

        lax.fori_loop(0, PER_GROUP, advance, (cs, sn), unroll=4)


def channelize_kernel(
    flag_ref,
    volt_hbm,
    band_hbm,
    delays_hbm,
    taper_hbm,
    outer_h_hbm,
    outer_l_hbm,
    twist_hbm,
    inner_h_hbm,
    inner_l_hbm,
    spread_hbm,
    section_hbm,
    swap_hbm,
    split_hbm,
    recv_ref,
    w_ref,
    section_ref,
    swap_ref,
    split_ref,
    volt_ref,
    band_ref,
    delays_ref,
    taper_ref,
    outer_h_ref,
    outer_l_ref,
    twist_ref,
    inner_h_ref,
    inner_l_ref,
    spread_ref,
    choice_ref,
    fh_ref,
    fl_ref,
    y_ref,
    o_ref,
    send_ref,
    pow_ref,
    load_sem,
    send_sem,
    recv_sem,
    own_sem,
    ready_sem,
    high_sem,
    all_sem,
):
    me, sec = lax.axis_index("stn"), lax.axis_index("sec")
    plane, place = me // PLANE, lax.rem(me, PLANE)
    barrier = pltpu.get_barrier_semaphore()
    loads = [
        pltpu.make_async_copy(src, dst, load_sem.at[n])
        for n, (src, dst) in enumerate(
            (
                (volt_hbm, volt_ref),
                (taper_hbm, taper_ref),
                (band_hbm, band_ref),
                (spread_hbm, spread_ref),
                (outer_h_hbm, outer_h_ref),
                (outer_l_hbm, outer_l_ref),
                (twist_hbm, twist_ref),
                (inner_h_hbm, inner_h_ref),
                (inner_l_hbm, inner_l_ref),
                (delays_hbm, delays_ref),
                (section_hbm, choice_ref),
                (swap_hbm, swap_ref),
                (split_hbm, split_ref),
            )
        )
    ]
    for load in loads:
        load.start()

    is_low = plane < HALF

    @pl.when(is_low)
    def _():
        for i in range(1, PLANE):
            other = plane * PLANE + lax.rem(place + i, PLANE)
            pl.semaphore_signal(barrier, inc=1, device_id=(other, sec), device_id_type=MESH)

    for i in range(1, SECTIONS):
        other = lax.rem(sec + i, SECTIONS)
        pl.semaphore_signal(barrier, inc=1, device_id=(me, other), device_id_type=MESH)
    for load in loads[:9]:
        load.wait()

    group = lax.broadcasted_iota(jnp.int32, (8, 128), 0)
    lane8 = lax.broadcasted_iota(jnp.int32, (8, 128), 1)
    spread_parts = []
    for q in range(3):
        inside = (lane8 + 128 * q >= 48 * group) & (lane8 + 128 * q < 48 * group + 48)
        tiles = [
            jnp.where(inside, band_ref[0:1, 384 * t + 128 * q : 384 * t + 128 * q + 128], 0.0)
            for t in range(16)
        ]
        spread_parts.append(jnp.concatenate(tiles, axis=0))
    band_h, band_l = split2(jnp.concatenate(spread_parts, axis=1))

    for part in range(2):
        for chunk in range(6):
            rows = slice(16 * chunk, 16 * chunk + 16)
            taps = [taper_ref[j, rows, :] for j in range(TAPS)]
            blocks = [
                volt_ref[part, 96 * n + 16 * chunk : 96 * n + 16 * chunk + 16, :].astype(jnp.float32)
                for n in range(FRAMES + TAPS - 1)
            ]
            for m in range(FRAMES):
                total = taps[0] * blocks[m]
                for j in range(1, TAPS):
                    total = total + taps[j] * blocks[m + j]
                high, low = split2(total)
                at = slice(96 * part + 16 * chunk, 96 * part + 16 * chunk + 16)
                fh_ref[at, 128 * m : 128 * m + 128] = high
                fl_ref[at, 128 * m : 128 * m + 128] = low

    cos, sin = twist_ref[0], twist_ref[1]
    for pair in range(FRAMES // 2):
        lanes = slice(256 * pair, 256 * pair + 256)
        fh = fh_ref[:, lanes]
        seg = dot_f32(outer_h_ref[...], fh, NN)
        seg = seg + dot_f32(outer_l_ref[...], fh, NN)
        seg = seg + dot_f32(outer_h_ref[...], fl_ref[:, lanes], NN)
        for half in range(2):
            m = 2 * pair + half
            for pol in range(POLS):
                sr = seg[96 * pol : 96 * pol + 48, 128 * half : 128 * half + 128]
                si = seg[96 * pol + 48 : 96 * pol + 96, 128 * half : 128 * half + 128]
                yr = sr * cos + si * sin
                yi = si * cos - sr * sin
                real_rows = pl.ds(m, 48, stride=12)
                imag_rows = pl.ds(FRAMES + m, 48, stride=12)
                y_ref[2 * pol, real_rows, :] = yr
                y_ref[2 * pol + 1, real_rows, :] = yi
                y_ref[2 * pol, imag_rows, :] = yi
                y_ref[2 * pol + 1, imag_rows, :] = -yr

    powers = [jnp.zeros((8, 128), jnp.float32) for _ in range(POLS)]
    for first, count in ((0, 2), (2, 2), (4, 1)):
        width = 128 * count
        depth = min(width, 576 - 128 * first)
        columns = spread_ref[:, 128 * first : 128 * first + width]
        spread = dot_f32(band_h, columns, NN) + dot_f32(band_l, columns, NN)
        for pol in range(POLS):
            y = jnp.concatenate(
                [y_ref[2 * pol + t, 128 * first : 128 * first + depth, :] for t in range(2)], axis=1
            )
            if depth < width:
                y = jnp.concatenate([y, jnp.zeros((width - depth, 256), jnp.float32)], axis=0)
            yh, yl = split2(y)
            out = dot_f32(inner_h_ref[...], yh, NT)
            out = out + dot_f32(inner_l_ref[...], yh, NT)
            out = out + dot_f32(inner_h_ref[...], yl, NT)
            out = out * spread
            square = out * out
            for t in range(count):
                piece = slice(128 * t, 128 * t + 128)
                o_ref[first + t, pl.ds(pol, 128, stride=2), :] = out[:, piece]
                powers[pol] = powers[pol] + jnp.sum(square[:, piece].reshape(16, 8, 128), axis=0)
    for j in range(4):
        send_ref[j] = o_ref[j].astype(jnp.bfloat16).reshape(128, 2, 128)
    lane = lax.broadcasted_iota(jnp.int32, (1, 128), 1)
    totals = [jnp.sum(p, keepdims=True) for p in powers]
    pow_ref[SECTIONS] = jnp.where(lane < 64, totals[0], totals[1])

    def at_place(z):
        return (z * PLANE + place, sec)

    @pl.when(is_low)
    def _():
        pl.semaphore_wait(barrier, PLANE - 1 + SECTIONS - 1 + plane)

        def greet_later(z, carry):
            pl.semaphore_signal(barrier, inc=1, device_id=at_place(z), device_id_type=MESH)
            return carry

        def greet_earlier(z, carry):
            pl.semaphore_signal(
                ready_sem.at[plane], inc=1, device_id=at_place(z), device_id_type=MESH
            )
            return carry

        lax.fori_loop(plane + 1, PLANES, greet_later, 0)
        lax.fori_loop(0, plane, greet_earlier, 0)

    @pl.when(jnp.logical_not(is_low))
    def _():
        pl.semaphore_wait(barrier, SECTIONS - 1 + HALF)

    def power_copy(j):
        return pltpu.make_async_remote_copy(
            src_ref=pow_ref.at[SECTIONS],
            dst_ref=pow_ref.at[sec],
            send_sem=send_sem.at[0],
            recv_sem=recv_sem.at[0],
            device_id=(me, lax.rem(sec + j, SECTIONS)),
            device_id_type=MESH,
        )

    for j in range(1, SECTIONS):
        power_copy(j).start()

    def block_copy(to, tiles):
        return pltpu.make_async_remote_copy(
            src_ref=send_ref.at[tiles, to],
            dst_ref=recv_ref.at[tiles, me],
            send_sem=send_sem.at[1],
            recv_sem=recv_sem.at[1],
            device_id=(to, sec),
            device_id_type=MESH,
        )

    body, tail, whole = pl.ds(0, 4), pl.ds(4, 1), pl.ds(0, 5)

    def send_plane(z, tiles, mates=False):
        for i in PLACES[: PLANE - 1] if mates else PLACES:
            block_copy(z * PLANE + lax.rem(place + i, PLANE), tiles).start()

    def send_low_half(tiles):
        def one(n, carry):
            send_plane(lax.rem(plane + n, HALF), tiles)
            return carry

        lax.fori_loop(0, HALF, one, 0)

    @pl.when(jnp.logical_not(is_low))
    def _():
        send_low_half(body)
        mirror = PLANES - 1 - plane
        for i in range(PLANE):
            other = mirror * PLANE + lax.rem(place + i, PLANE)
            pl.semaphore_signal(high_sem, inc=1, device_id=(other, sec), device_id_type=MESH)

    def bytes_of(ref, slot):
        return pltpu.make_async_remote_copy(
            src_ref=ref,
            dst_ref=ref,
            send_sem=send_sem.at[slot],
            recv_sem=recv_sem.at[slot],
            device_id=(me, sec),
            device_id_type=MESH,
        )

    three = bytes_of(pow_ref.at[pl.ds(0, SECTIONS - 1)], 0)
    three.wait_send()
    three.wait_recv()
    mine = lax.broadcasted_iota(jnp.int32, (1, 128), 1) * 0 + sec
    total = pow_ref[SECTIONS]
    for other in range(SECTIONS):
        total = total + jnp.where(mine == other, 0.0, pow_ref[other])
    mean = total * (1.0 / (SECTIONS * FRAMES * NCH))
    gain = jnp.where(flag_ref[0] == 1, 0.0, 1.0 / jnp.sqrt(mean + 1e-05))
    g0 = gain.astype(jnp.bfloat16).astype(jnp.float32)
    g1 = (gain - g0).astype(jnp.bfloat16).astype(jnp.float32)
    g2 = gain - g0 - g1
    row = lax.broadcasted_iota(jnp.int32, (8, 128), 0)
    col = lax.broadcasted_iota(jnp.int32, (8, 128), 1)
    patch = jnp.zeros((8, 128), jnp.float32)
    for at, g in ((0, g0), (1, g1), (2, g2)):
        pair = jnp.where(row % 2 == 0, g[:, 0:1], g[:, 64:65])
        patch = jnp.where(col == GAIN_LANE + at, pair, patch)
    patch = jnp.broadcast_to(patch[None], (INPUTS // 8, 8, 128)).reshape(INPUTS, 128)
    wide = lax.broadcasted_iota(jnp.int32, (INPUTS, 128), 1)
    tile = jnp.where(wide < GAIN_LANE, o_ref[4], patch)
    send_ref[4] = tile.astype(jnp.bfloat16).reshape(128, 2, 128)
    def send_ready(z):
        pl.semaphore_wait(ready_sem.at[z], 1)
        send_plane(z, whole)

    @pl.when(is_low)
    def _():
        def earlier(z, carry):
            send_plane(z, whole)
            return carry

        def later(z, carry):
            send_ready(z)
            return carry

        send_plane(plane, whole, mates=True)
        lax.fori_loop(0, plane, earlier, 0)
        lax.fori_loop(plane + 1, HALF, later, 0)

    @pl.when(jnp.logical_not(is_low))
    def _():
        send_low_half(tail)

    own = pltpu.make_async_copy(send_ref.at[:, me], recv_ref.at[:, me], own_sem)
    own.start()
    for load in loads[10:]:
        load.wait()
    section_ref[...] = jnp.full((8, 128), choice_ref[sec]).astype(jnp.float32)
    loads[9].wait()
    make_weights(delays_ref[...], sec * NCH + me * PER_GROUP, w_ref)

    @pl.when(is_low)
    def _():
        mirror = PLANES - 1 - plane
        pl.semaphore_wait(high_sem, PLANE)
        for i in range(1, HALF):
            other = lax.rem(plane + i, HALF)
            pl.semaphore_signal(
                ready_sem.at[mirror], inc=1, device_id=at_place(other), device_id_type=MESH
            )
        send_plane(mirror, whole)

        def other_high(n, carry):
            send_ready(HALF + lax.rem(mirror + n, HALF))
            return carry

        lax.fori_loop(1, HALF, other_high, 0)
        pl.semaphore_signal(all_sem, inc=1, device_id=at_place(mirror), device_id_type=MESH)

    @pl.when(jnp.logical_not(is_low))
    def _():
        pl.semaphore_wait(all_sem, 1)
        send_plane(plane, whole, mates=True)

        def mates(n, carry):
            send_plane(HALF + lax.rem(plane + n, HALF), whole)
            return carry

        lax.fori_loop(1, HALF, mates, 0)

    own.wait()
    sent = bytes_of(send_ref.at[:, pl.ds(0, STATIONS - 1)], 1)
    sent.wait_send()
    landed = bytes_of(recv_ref.at[:, pl.ds(0, STATIONS - 1)], 1)
    landed.wait_recv()


def channelize(volts, band, delays, flags, section):
    outer_h, outer_l = split_const(outer_table())
    inner_h, inner_l = split_const(inner_table())
    inputs = [
        volts,
        band,
        delays,
        jnp.asarray(taper_table()),
        jnp.asarray(outer_h),
        jnp.asarray(outer_l),
        jnp.asarray(twist_tables()),
        jnp.asarray(inner_h),
        jnp.asarray(inner_l),
        jnp.asarray(spread_table(), jnp.bfloat16),
    ]
    swap = jnp.asarray(swap_table(), jnp.bfloat16)
    split = jnp.asarray(split_table(), jnp.bfloat16)
    operands = [
        pltpu.with_memory_space_constraint(x, pltpu.HBM)
        for x in inputs + [section, swap, split]
    ]
    vmem = pl.BlockSpec(memory_space=pltpu.VMEM)
    return pl.pallas_call(
        channelize_kernel,
        out_shape=(
            pltpu.VMEM((5, STATIONS, POLS, 128), jnp.bfloat16),
            pltpu.VMEM((PER_GROUP, INPUTS, BEAMS), jnp.bfloat16),
            pltpu.VMEM((8, 128), jnp.float32),
            pltpu.VMEM(swap.shape, swap.dtype),
            pltpu.VMEM(split.shape, split.dtype),
        ),
        in_specs=[pl.BlockSpec(memory_space=pltpu.SMEM)]
        + [pl.BlockSpec(memory_space=pltpu.HBM)] * len(operands),
        out_specs=(vmem,) * 5,
        scratch_shapes=[pltpu.VMEM(x.shape, x.dtype) for x in inputs]
        + [
            pltpu.SMEM(section.shape, section.dtype),
            pltpu.VMEM((192, 768), jnp.bfloat16),
            pltpu.VMEM((192, 768), jnp.bfloat16),
            pltpu.VMEM((4, 576, 128), jnp.float32),
            pltpu.VMEM((5, 256, 128), jnp.float32),
            pltpu.VMEM((5, STATIONS, POLS, 128), jnp.bfloat16),
            pltpu.VMEM((5, 1, 128), jnp.float32),
            pltpu.SemaphoreType.DMA((len(operands),)),
            pltpu.SemaphoreType.DMA((2,)),
            pltpu.SemaphoreType.DMA((2,)),
            pltpu.SemaphoreType.DMA,
            pltpu.SemaphoreType.REGULAR((PLANES,)),
            pltpu.SemaphoreType.REGULAR,
            pltpu.SemaphoreType.REGULAR,
        ],
        compiler_params=pltpu.CompilerParams(
            collective_id=0, has_side_effects=True, vmem_limit_bytes=24 << 20
        ),
        name="channelize",
    )(flags, *operands)


def per_device(voltages, bandpass, station_flags, delays, section):
    volts = voltages.reshape(2, POLS, 624, 128).transpose(0, 2, 1, 3).reshape(2, 1248, 128)
    turned, weights, choice, swap, split = channelize(
        volts, bandpass, delays, station_flags, section
    )
    vis, tied = finish(choice, weights, turned.reshape(5, INPUTS, 128), swap, split)
    return (vis[None], tied[None])


def solution(mesh):
    return jax.shard_map(
        per_device,
        mesh=mesh,
        in_specs=(P(None, "stn", "sec", None, None), P("sec", None), P("stn"), P(), P()),
        out_specs=(P("sec", "stn", None, None), P("sec", "stn", None, None, None, None)),
        check_vma=False,
    )
```

```python
import functools
import math

import jax
import jax.numpy as jnp
import numpy as np
from jax import lax
from jax.experimental import pallas as pl
from jax.experimental.pallas import tpu as pltpu
from jax.sharding import PartitionSpec as P

POLS = 2
NCH = 6144
TAPS = 8
FRAMES = 6
AVG = 12
BEAMS = 256
STATIONS = 128
INPUTS = STATIONS * POLS
PER_GROUP = 48
VIS_LOCAL = PER_GROUP // AVG
BLOCK = AVG * 2 * FRAMES
PERIOD = 65536
GAIN_LANE = 64
PLANES = 8
PLANE = STATIONS // PLANES
SECTIONS = 4
HALF = PLANES // 2
PLACES = (8, 9, 6, 7, 10, 11, 4, 5, 12, 13, 2, 3, 14, 15, 1, 0)
MESH = pl.DeviceIdType.MESH

NT = (((1,), (1,)), ((), ()))
NN = (((1,), (0,)), ((), ()))


def dot_f32(lhs, rhs, dims):
    return lax.dot_general(lhs, rhs, dims, preferred_element_type=jnp.float32)


def swap_table():
    table = np.zeros((VIS_LOCAL, INPUTS, INPUTS), np.float32)
    for v in range(VIS_LOCAL):
        for q in range(BLOCK):
            real = q % 12 < 6
            table[v, 16 * v + q, 16 * v + (q + 6 if real else q - 6)] = -1.0 if real else 1.0
    return table


def split_table():
    table = np.zeros((INPUTS, INPUTS), np.float32)
    for pol in range(POLS):
        for station in range(STATIONS):
            table[pol * STATIONS + station, station * POLS + pol] = 1.0
    return table


def finish_kernel(
    section_ref,
    w_ref,
    r_ref,
    swap_ref,
    split_ref,
    vis_hbm,
    beam_hbm,
    vis_ref,
    beam_ref,
    xl_ref,
    xs_ref,
    out_sem,
    zero_sem,
):
    is_beam = jnp.max(section_ref[...]) == 1.0

    @pl.when(jnp.logical_not(is_beam))
    def _():
        beam_ref[...] = jnp.zeros_like(beam_ref)
        zero = pltpu.make_async_copy(beam_ref, beam_hbm, zero_sem)
        zero.start()
        copies = []
        last = r_ref[VIS_LOCAL]
        gain_col = jnp.sum(
            last[:, GAIN_LANE : GAIN_LANE + 3].astype(jnp.float32), axis=1, keepdims=True
        )
        gain_col = gain_col * (1.0 / math.sqrt(FRAMES * AVG))
        lane8 = lax.broadcasted_iota(jnp.int32, (8, 128), 1)
        pick = jnp.where((lane8 >= GAIN_LANE) & (lane8 < GAIN_LANE + 3), 1.0, 0.0)
        gain_row = dot_f32(pick.astype(jnp.bfloat16), last, NT)[0:1, :]
        rows = lax.broadcasted_iota(jnp.int32, (INPUTS, INPUTS), 0)
        cols = lax.broadcasted_iota(jnp.int32, (INPUTS, INPUTS), 1)
        for v in range(VIS_LOCAL):
            left = jnp.concatenate([r_ref[v], r_ref[v + 1]], axis=1)
            inside = (cols >= 16 * v) & (cols < 16 * v + BLOCK)
            same = jnp.where(inside, left.astype(jnp.float32), 0.0).astype(jnp.bfloat16)
            other = dot_f32(left, swap_ref[v], NT).astype(jnp.bfloat16)
            real = dot_f32(left, same, NT)
            imag = dot_f32(left, other, NT)
            packed = jnp.where(rows <= cols, real, imag)
            vis_ref[v] = (packed * gain_col * gain_row).astype(jnp.bfloat16)
            copies.append(pltpu.make_async_copy(vis_ref.at[v], vis_hbm.at[v], out_sem.at[v]))
            copies[v].start()
        for copy in copies:
            copy.wait()
        zero.wait()

    @pl.when(is_beam)
    def _():
        vis_ref[...] = jnp.zeros_like(vis_ref)
        zero = pltpu.make_async_copy(vis_ref, vis_hbm, zero_sem)
        zero.start()
        gain = None
        for j in range(VIS_LOCAL, -1, -1):
            part = dot_f32(split_ref[...], r_ref[j], NN)
            if gain is None:
                gain = jnp.sum(part[:, GAIN_LANE : GAIN_LANE + 3], axis=1, keepdims=True)
            xs_ref[j] = (part * gain).astype(jnp.bfloat16)
        q_row = lax.broadcasted_iota(jnp.int32, (BLOCK, INPUTS), 0)
        q_col = lax.broadcasted_iota(jnp.int32, (BLOCK, INPUTS), 1)
        scale = 1.0 / math.sqrt(STATIONS)
        copies = []
        for v in range(VIS_LOCAL):
            window = jnp.concatenate([xs_ref[v], xs_ref[v + 1]], axis=1)
            keep = jnp.where(q_col == q_row + 16 * v, 1.0, 0.0).astype(jnp.bfloat16)
            plain = dot_f32(keep, window, NT)
            other = dot_f32(swap_ref[v, 16 * v : 16 * v + BLOCK, :], window, NT)
            for pol in range(POLS):
                rows = pl.ds(2 * BLOCK * v + pol, BLOCK, stride=2)
                half = slice(128 * pol, 128 * pol + 128)
                xl_ref[0, rows, :] = plain[:, half]
                xl_ref[1, rows, :] = other[:, half]
            for k in range(AVG * v, AVG * v + AVG):
                rows = slice(24 * k, 24 * k + 24)
                left = jnp.concatenate([xl_ref[0, rows, :], xl_ref[1, rows, :]], axis=1)
                out = dot_f32(left.astype(jnp.bfloat16), w_ref[k], NN) * scale
                beam_ref[k] = out.astype(jnp.bfloat16).reshape(2 * FRAMES, POLS, BEAMS)
            part = pl.ds(AVG * v, AVG)
            copies.append(
                pltpu.make_async_copy(beam_ref.at[part], beam_hbm.at[part], out_sem.at[v])
            )
            copies[v].start()
        for copy in copies:
            copy.wait()
        zero.wait()


def finish(section, weights, received, swap, split):
    vmem = pl.BlockSpec(memory_space=pltpu.VMEM)
    anywhere = pl.BlockSpec(memory_space=pl.ANY)
    vis_shape = (VIS_LOCAL, INPUTS, INPUTS)
    beam_shape = (PER_GROUP, 2 * FRAMES, POLS, BEAMS)
    vis, beam = pl.pallas_call(
        finish_kernel,
        out_shape=(
            jax.ShapeDtypeStruct(vis_shape, jnp.bfloat16),
            jax.ShapeDtypeStruct(beam_shape, jnp.bfloat16),
        ),
        in_specs=[vmem] * 5,
        out_specs=(anywhere, anywhere),
        scratch_shapes=[
            pltpu.VMEM(vis_shape, jnp.bfloat16),
            pltpu.VMEM(beam_shape, jnp.bfloat16),
            pltpu.VMEM((2, PER_GROUP * 24, 128), jnp.float32),
            pltpu.VMEM((5, INPUTS, 128), jnp.bfloat16),
            pltpu.SemaphoreType.DMA((4,)),
            pltpu.SemaphoreType.DMA,
        ],
        compiler_params=pltpu.CompilerParams(vmem_limit_bytes=24 << 20),
        name="finish",
    )(section, weights, received, swap, split)
    tied = beam.reshape(PER_GROUP, 2, FRAMES, POLS, BEAMS).transpose(0, 1, 3, 2, 4)
    return vis, tied


def split2(value):
    high = value.astype(jnp.bfloat16)
    return high, (value - high.astype(jnp.float32)).astype(jnp.bfloat16)


def split_const(table):
    table = np.asarray(table, np.float32)
    high = table.astype(jnp.bfloat16)
    return high, (table - high.astype(np.float32)).astype(jnp.bfloat16)


def taper_table():
    index = np.arange(TAPS * NCH, dtype=np.float64)
    offset = (index + 0.5 - TAPS * NCH / 2.0) / NCH
    window = 0.5 - 0.5 * np.cos(2.0 * np.pi * (index + 0.5) / (TAPS * NCH))
    table = (np.sinc(offset) * window).reshape(TAPS, PER_GROUP, 1, 128)
    table = np.broadcast_to(table, (TAPS, PER_GROUP, POLS, 128))
    return table.reshape(TAPS, 2 * PER_GROUP, 128).astype(np.float32)


def outer_table():
    angle = 2.0 * np.pi * (np.outer(np.arange(48), np.arange(48)) % 48) / 48.0
    cos, sin = np.cos(angle), np.sin(angle)
    table = np.zeros((POLS, 2, 48, 2, 48, POLS))
    for pol in range(POLS):
        table[pol, 0, :, 0, :, pol] = cos
        table[pol, 0, :, 1, :, pol] = sin
        table[pol, 1, :, 0, :, pol] = -sin
        table[pol, 1, :, 1, :, pol] = cos
    return table.reshape(192, 192)


def twist_tables():
    angle = 2.0 * np.pi * np.outer(np.arange(48), np.arange(128)) / NCH
    return np.stack([np.cos(angle), np.sin(angle)]).astype(np.float32)


def inner_table():
    angle = 2.0 * np.pi * (np.outer(np.arange(128), np.arange(128)) % 128) / 128.0
    return np.concatenate([np.cos(angle), np.sin(angle)], axis=1)


def spread_table():
    row, col = np.arange(384)[:, None], np.arange(640)[None, :]
    return ((row % 48 == col // 12) & (col < 576)).astype(np.float32)


def make_weights(delays, first, w_ref):
    delay = delays.astype(jnp.float32).T.astype(jnp.int32)
    turn = 2.0 * math.pi / PERIOD
    start = (delay * first & (PERIOD - 1)).astype(jnp.float32) * turn
    step = delay.astype(jnp.float32) * turn
    state = (jnp.cos(start), jnp.sin(start), jnp.cos(step), jnp.sin(step))
    for sb in range(8):
        cs, sn, dc, ds = (t[16 * sb : 16 * sb + 16] for t in state)

        def advance(k, carry):
            c, s = carry
            w_ref[k, 16 * sb : 16 * sb + 16, :] = c.astype(jnp.bfloat16)
            w_ref[k, 128 + 16 * sb : 128 + 16 * sb + 16, :] = s.astype(jnp.bfloat16)
            return (c * dc - s * ds, c * ds + s * dc)

        lax.fori_loop(0, PER_GROUP, advance, (cs, sn), unroll=4)


def channelize_kernel(
    flag_ref,
    volt_hbm,
    band_hbm,
    delays_hbm,
    taper_hbm,
    outer_hbm,
    twist_hbm,
    inner_hbm,
    spread_hbm,
    section_hbm,
    swap_hbm,
    split_hbm,
    recv_ref,
    w_ref,
    section_ref,
    swap_ref,
    split_ref,
    volt_ref,
    band_ref,
    delays_ref,
    taper_ref,
    outer_ref,
    twist_ref,
    inner_ref,
    spread_ref,
    choice_ref,
    f_ref,
    y_ref,
    o_ref,
    send_ref,
    pow_ref,
    load_sem,
    send_sem,
    recv_sem,
    own_sem,
    ready_sem,
    high_sem,
    all_sem,
):
    me, sec = lax.axis_index("stn"), lax.axis_index("sec")
    plane, place = me // PLANE, lax.rem(me, PLANE)
    barrier = pltpu.get_barrier_semaphore()
    loads = [
        pltpu.make_async_copy(src, dst, load_sem.at[n])
        for n, (src, dst) in enumerate(
            (
                (taper_hbm, taper_ref),
                (volt_hbm.at[0], volt_ref.at[0]),
                (volt_hbm.at[1], volt_ref.at[1]),
                (band_hbm, band_ref),
                (spread_hbm, spread_ref),
                (outer_hbm, outer_ref),
                (twist_hbm, twist_ref),
                (inner_hbm, inner_ref),
                (delays_hbm, delays_ref),
                (section_hbm, choice_ref),
                (swap_hbm, swap_ref),
                (split_hbm, split_ref),
            )
        )
    ]
    for load in loads:
        load.start()

    is_low = plane < HALF

    @pl.when(is_low)
    def _():
        for i in range(1, PLANE):
            other = plane * PLANE + lax.rem(place + i, PLANE)
            pl.semaphore_signal(barrier, inc=1, device_id=(other, sec), device_id_type=MESH)

    for i in range(1, SECTIONS):
        other = lax.rem(sec + i, SECTIONS)
        pl.semaphore_signal(barrier, inc=1, device_id=(me, other), device_id_type=MESH)
    loads[0].wait()
    for part in range(2):
        loads[1 + part].wait()
        if part == 1:
            for load in loads[3:8]:
                load.wait()
        for chunk in range(6):
            rows = slice(16 * chunk, 16 * chunk + 16)
            taps = [taper_ref[j, rows, :] for j in range(TAPS)]
            blocks = [
                volt_ref[part, 96 * n + 16 * chunk : 96 * n + 16 * chunk + 16, :].astype(jnp.float32)
                for n in range(FRAMES + TAPS - 1)
            ]
            at = 96 * part + 16 * chunk
            for m in range(FRAMES):
                total = taps[0] * blocks[m]
                for j in range(1, TAPS):
                    total = total + taps[j] * blocks[m + j]
                high, low = split2(total)
                lanes = slice(128 * m, 128 * m + 128)
                f_ref[at : at + 16, lanes] = high
                f_ref[192 + at : 192 + at + 16, lanes] = high
                f_ref[384 + at : 384 + at + 16, lanes] = low

    group = lax.broadcasted_iota(jnp.int32, (8, 128), 0)
    lane8 = lax.broadcasted_iota(jnp.int32, (8, 128), 1)
    spread_parts = []
    for q in range(3):
        inside = (lane8 + 128 * q >= 48 * group) & (lane8 + 128 * q < 48 * group + 48)
        tiles = [
            jnp.where(inside, band_ref[0:1, 384 * t + 128 * q : 384 * t + 128 * q + 128], 0.0)
            for t in range(16)
        ]
        spread_parts.append(jnp.concatenate(tiles, axis=0))
    band_h, band_l = split2(jnp.concatenate(spread_parts, axis=1))

    cos, sin = twist_ref[0], twist_ref[1]
    for pair in range(FRAMES // 2):
        lanes = slice(256 * pair, 256 * pair + 256)
        seg = dot_f32(outer_ref[...], f_ref[:, lanes], NN)
        for half in range(2):
            m = 2 * pair + half
            for pol in range(POLS):
                sr = seg[96 * pol : 96 * pol + 48, 128 * half : 128 * half + 128]
                si = seg[96 * pol + 48 : 96 * pol + 96, 128 * half : 128 * half + 128]
                yr = sr * cos + si * sin
                yi = si * cos - sr * sin
                real_rows = pl.ds(m, 48, stride=12)
                imag_rows = pl.ds(FRAMES + m, 48, stride=12)
                y_ref[2 * pol, real_rows, :] = yr
                y_ref[2 * pol + 1, real_rows, :] = yi
                y_ref[2 * pol, imag_rows, :] = yi
                y_ref[2 * pol + 1, imag_rows, :] = -yr

    powers = [jnp.zeros((8, 128), jnp.float32) for _ in range(POLS)]
    for first, count in ((0, 2), (2, 2), (4, 1)):
        width = 128 * count
        depth = min(width, 576 - 128 * first)
        columns = spread_ref[:, 128 * first : 128 * first + width]
        spread = dot_f32(band_h, columns, NN) + dot_f32(band_l, columns, NN)
        for pol in range(POLS):
            y = jnp.concatenate(
                [y_ref[2 * pol + t, 128 * first : 128 * first + depth, :] for t in range(2)], axis=1
            )
            if depth < width:
                y = jnp.concatenate([y, jnp.zeros((width - depth, 256), jnp.float32)], axis=0)
            yh, yl = split2(y)
            out = dot_f32(inner_ref[...], jnp.concatenate([yh, yh, yl], axis=1), NT)
            out = out * spread
            square = out * out
            for t in range(count):
                piece = slice(128 * t, 128 * t + 128)
                o_ref[first + t, pl.ds(pol, 128, stride=2), :] = out[:, piece]
                powers[pol] = powers[pol] + jnp.sum(square[:, piece].reshape(16, 8, 128), axis=0)
    lane = lax.broadcasted_iota(jnp.int32, (1, 128), 1)
    totals = [jnp.sum(p, keepdims=True) for p in powers]
    pow_ref[SECTIONS] = jnp.where(lane < 64, totals[0], totals[1])

    def at_place(z):
        return (z * PLANE + place, sec)

    @pl.when(is_low)
    def _():
        pl.semaphore_wait(barrier, PLANE - 1 + SECTIONS - 1 + plane)

        def greet_later(z, carry):
            pl.semaphore_signal(barrier, inc=1, device_id=at_place(z), device_id_type=MESH)
            return carry

        def greet_earlier(z, carry):
            pl.semaphore_signal(
                ready_sem.at[plane], inc=1, device_id=at_place(z), device_id_type=MESH
            )
            return carry

        lax.fori_loop(plane + 1, PLANES, greet_later, 0)
        lax.fori_loop(0, plane, greet_earlier, 0)

    @pl.when(jnp.logical_not(is_low))
    def _():
        pl.semaphore_wait(barrier, SECTIONS - 1 + HALF)

    def power_copy(j):
        return pltpu.make_async_remote_copy(
            src_ref=pow_ref.at[SECTIONS],
            dst_ref=pow_ref.at[sec],
            send_sem=send_sem.at[0],
            recv_sem=recv_sem.at[0],
            device_id=(me, lax.rem(sec + j, SECTIONS)),
            device_id_type=MESH,
        )

    for j in range(1, SECTIONS):
        power_copy(j).start()
    for j in range(4):
        send_ref[j] = o_ref[j].astype(jnp.bfloat16).reshape(128, 2, 128)

    def block_copy(to, tiles):
        return pltpu.make_async_remote_copy(
            src_ref=send_ref.at[tiles, to],
            dst_ref=recv_ref.at[tiles, me],
            send_sem=send_sem.at[1],
            recv_sem=recv_sem.at[1],
            device_id=(to, sec),
            device_id_type=MESH,
        )

    body, tail, whole = pl.ds(0, 4), pl.ds(4, 1), pl.ds(0, 5)

    def send_plane(z, tiles, mates=False):
        for i in PLACES[: PLANE - 1] if mates else PLACES:
            block_copy(z * PLANE + lax.rem(place + i, PLANE), tiles).start()

    def send_low_half(tiles):
        def one(n, carry):
            send_plane(lax.rem(plane + n, HALF), tiles)
            return carry

        lax.fori_loop(0, HALF, one, 0)

    @pl.when(jnp.logical_not(is_low))
    def _():
        send_low_half(body)
        mirror = PLANES - 1 - plane
        for i in range(PLANE):
            other = mirror * PLANE + lax.rem(place + i, PLANE)
            pl.semaphore_signal(high_sem, inc=1, device_id=(other, sec), device_id_type=MESH)

    def bytes_of(ref, slot):
        return pltpu.make_async_remote_copy(
            src_ref=ref,
            dst_ref=ref,
            send_sem=send_sem.at[slot],
            recv_sem=recv_sem.at[slot],
            device_id=(me, sec),
            device_id_type=MESH,
        )

    three = bytes_of(pow_ref.at[pl.ds(0, SECTIONS - 1)], 0)
    three.wait_send()
    three.wait_recv()
    mine = lax.broadcasted_iota(jnp.int32, (1, 128), 1) * 0 + sec
    total = pow_ref[SECTIONS]
    for other in range(SECTIONS):
        total = total + jnp.where(mine == other, 0.0, pow_ref[other])
    mean = total * (1.0 / (SECTIONS * FRAMES * NCH))
    gain = jnp.where(flag_ref[0] == 1, 0.0, 1.0 / jnp.sqrt(mean + 1e-05))
    g0 = gain.astype(jnp.bfloat16).astype(jnp.float32)
    g1 = (gain - g0).astype(jnp.bfloat16).astype(jnp.float32)
    g2 = gain - g0 - g1
    row = lax.broadcasted_iota(jnp.int32, (8, 128), 0)
    col = lax.broadcasted_iota(jnp.int32, (8, 128), 1)
    patch = jnp.zeros((8, 128), jnp.float32)
    for at, g in ((0, g0), (1, g1), (2, g2)):
        pair = jnp.where(row % 2 == 0, g[:, 0:1], g[:, 64:65])
        patch = jnp.where(col == GAIN_LANE + at, pair, patch)
    patch = jnp.broadcast_to(patch[None], (INPUTS // 8, 8, 128)).reshape(INPUTS, 128)
    wide = lax.broadcasted_iota(jnp.int32, (INPUTS, 128), 1)
    tile = jnp.where(wide < GAIN_LANE, o_ref[4], patch)
    send_ref[4] = tile.astype(jnp.bfloat16).reshape(128, 2, 128)
    def send_ready(z):
        pl.semaphore_wait(ready_sem.at[z], 1)
        send_plane(z, whole)

    @pl.when(is_low)
    def _():
        def earlier(z, carry):
            send_plane(z, whole)
            return carry

        def later(z, carry):
            send_ready(z)
            return carry

        send_plane(plane, whole, mates=True)
        lax.fori_loop(0, plane, earlier, 0)
        lax.fori_loop(plane + 1, HALF, later, 0)

    @pl.when(jnp.logical_not(is_low))
    def _():
        send_low_half(tail)

    own = pltpu.make_async_copy(send_ref.at[:, me], recv_ref.at[:, me], own_sem)
    own.start()
    for load in loads[8:]:
        load.wait()
    section_ref[...] = jnp.full((8, 128), choice_ref[sec]).astype(jnp.float32)
    make_weights(delays_ref[...], sec * NCH + me * PER_GROUP, w_ref)

    @pl.when(is_low)
    def _():
        mirror = PLANES - 1 - plane
        pl.semaphore_wait(high_sem, PLANE)
        for i in range(1, HALF):
            other = lax.rem(plane + i, HALF)
            pl.semaphore_signal(
                ready_sem.at[mirror], inc=1, device_id=at_place(other), device_id_type=MESH
            )
        send_plane(mirror, whole)

        def other_high(n, carry):
            send_ready(HALF + lax.rem(mirror + n, HALF))
            return carry

        lax.fori_loop(1, HALF, other_high, 0)
        pl.semaphore_signal(all_sem, inc=1, device_id=at_place(mirror), device_id_type=MESH)

    @pl.when(jnp.logical_not(is_low))
    def _():
        pl.semaphore_wait(all_sem, 1)
        send_plane(plane, whole, mates=True)

        def mates(n, carry):
            send_plane(HALF + lax.rem(plane + n, HALF), whole)
            return carry

        lax.fori_loop(1, HALF, mates, 0)

    own.wait()
    sent = bytes_of(send_ref.at[:, pl.ds(0, STATIONS - 1)], 1)
    sent.wait_send()
    landed = bytes_of(recv_ref.at[:, pl.ds(0, STATIONS - 1)], 1)
    landed.wait_recv()


def channelize(volts, band, delays, flags, section):
    outer_h, outer_l = split_const(outer_table())
    inner_h, inner_l = split_const(inner_table())
    inputs = [
        volts,
        band,
        delays,
        jnp.asarray(taper_table()),
        jnp.asarray(np.concatenate([outer_h, outer_l, outer_h], axis=1)),
        jnp.asarray(twist_tables()),
        jnp.asarray(np.concatenate([inner_h, inner_l, inner_h], axis=1)),
        jnp.asarray(spread_table(), jnp.bfloat16),
    ]
    swap = jnp.asarray(swap_table(), jnp.bfloat16)
    split = jnp.asarray(split_table(), jnp.bfloat16)
    operands = [
        pltpu.with_memory_space_constraint(x, pltpu.HBM)
        for x in inputs + [section, swap, split]
    ]
    vmem = pl.BlockSpec(memory_space=pltpu.VMEM)
    return pl.pallas_call(
        channelize_kernel,
        out_shape=(
            pltpu.VMEM((5, STATIONS, POLS, 128), jnp.bfloat16),
            pltpu.VMEM((PER_GROUP, INPUTS, BEAMS), jnp.bfloat16),
            pltpu.VMEM((8, 128), jnp.float32),
            pltpu.VMEM(swap.shape, swap.dtype),
            pltpu.VMEM(split.shape, split.dtype),
        ),
        in_specs=[pl.BlockSpec(memory_space=pltpu.SMEM)]
        + [pl.BlockSpec(memory_space=pltpu.HBM)] * len(operands),
        out_specs=(vmem,) * 5,
        scratch_shapes=[pltpu.VMEM(x.shape, x.dtype) for x in inputs]
        + [
            pltpu.SMEM(section.shape, section.dtype),
            pltpu.VMEM((576, 768), jnp.bfloat16),
            pltpu.VMEM((4, 576, 128), jnp.float32),
            pltpu.VMEM((5, 256, 128), jnp.float32),
            pltpu.VMEM((5, STATIONS, POLS, 128), jnp.bfloat16),
            pltpu.VMEM((5, 1, 128), jnp.float32),
            pltpu.SemaphoreType.DMA((len(operands) + 1,)),
            pltpu.SemaphoreType.DMA((2,)),
            pltpu.SemaphoreType.DMA((2,)),
            pltpu.SemaphoreType.DMA,
            pltpu.SemaphoreType.REGULAR((PLANES,)),
            pltpu.SemaphoreType.REGULAR,
            pltpu.SemaphoreType.REGULAR,
        ],
        compiler_params=pltpu.CompilerParams(
            collective_id=0, has_side_effects=True, vmem_limit_bytes=24 << 20
        ),
        name="channelize",
    )(flags, *operands)


def per_device(voltages, bandpass, station_flags, delays, section):
    volts = voltages.reshape(2, POLS, 624, 128).transpose(0, 2, 1, 3).reshape(2, 1248, 128)
    turned, weights, choice, swap, split = channelize(
        volts, bandpass, delays, station_flags, section
    )
    vis, tied = finish(choice, weights, turned.reshape(5, INPUTS, 128), swap, split)
    return (vis[None], tied[None])


def solution(mesh):
    return jax.shard_map(
        per_device,
        mesh=mesh,
        in_specs=(P(None, "stn", "sec", None, None), P("sec", None), P("stn"), P(), P()),
        out_specs=(P("sec", "stn", None, None), P("sec", "stn", None, None, None, None)),
        check_vma=False,
    )
```

```python
import functools
import math

import jax
import jax.numpy as jnp
import numpy as np
from jax import lax
from jax.experimental import pallas as pl
from jax.experimental.pallas import tpu as pltpu
from jax.sharding import PartitionSpec as P

POLS = 2
NCH = 6144
TAPS = 8
FRAMES = 6
AVG = 12
BEAMS = 256
STATIONS = 128
INPUTS = STATIONS * POLS
PER_GROUP = 48
VIS_LOCAL = PER_GROUP // AVG
BLOCK = AVG * 2 * FRAMES
PERIOD = 65536
GAIN_LANE = 64
PLANES = 8
PLANE = STATIONS // PLANES
SECTIONS = 4
HALF = PLANES // 2
PLACES = (8, 9, 6, 7, 10, 11, 4, 5, 12, 13, 2, 3, 14, 15, 1, 0)
MESH = pl.DeviceIdType.MESH

NT = (((1,), (1,)), ((), ()))
NN = (((1,), (0,)), ((), ()))


def dot_f32(lhs, rhs, dims):
    return lax.dot_general(lhs, rhs, dims, preferred_element_type=jnp.float32)


def swap_table():
    table = np.zeros((VIS_LOCAL, INPUTS, INPUTS), np.float32)
    for v in range(VIS_LOCAL):
        for q in range(BLOCK):
            real = q % 12 < 6
            table[v, 16 * v + q, 16 * v + (q + 6 if real else q - 6)] = -1.0 if real else 1.0
    return table


def split_table():
    table = np.zeros((INPUTS, INPUTS), np.float32)
    for pol in range(POLS):
        for station in range(STATIONS):
            table[pol * STATIONS + station, station * POLS + pol] = 1.0
    return table


def finish_kernel(
    section_ref,
    w_ref,
    r_ref,
    swap_ref,
    split_ref,
    vis_hbm,
    beam_hbm,
    vis_ref,
    beam_ref,
    xl_ref,
    xs_ref,
    out_sem,
    zero_sem,
):
    is_beam = jnp.max(section_ref[...]) == 1.0

    @pl.when(jnp.logical_not(is_beam))
    def _():
        beam_ref[...] = jnp.zeros_like(beam_ref)
        zero = pltpu.make_async_copy(beam_ref, beam_hbm, zero_sem)
        zero.start()
        copies = []
        last = r_ref[VIS_LOCAL]
        gain_col = jnp.sum(
            last[:, GAIN_LANE : GAIN_LANE + 3].astype(jnp.float32), axis=1, keepdims=True
        )
        gain_col = gain_col * (1.0 / math.sqrt(FRAMES * AVG))
        lane8 = lax.broadcasted_iota(jnp.int32, (8, 128), 1)
        pick = jnp.where((lane8 >= GAIN_LANE) & (lane8 < GAIN_LANE + 3), 1.0, 0.0)
        gain_row = dot_f32(pick.astype(jnp.bfloat16), last, NT)[0:1, :]
        rows = lax.broadcasted_iota(jnp.int32, (INPUTS, INPUTS), 0)
        cols = lax.broadcasted_iota(jnp.int32, (INPUTS, INPUTS), 1)
        for v in range(VIS_LOCAL):
            left = jnp.concatenate([r_ref[v], r_ref[v + 1]], axis=1)
            inside = (cols >= 16 * v) & (cols < 16 * v + BLOCK)
            same = jnp.where(inside, left.astype(jnp.float32), 0.0).astype(jnp.bfloat16)
            other = dot_f32(left, swap_ref[v], NT).astype(jnp.bfloat16)
            real = dot_f32(left, same, NT)
            imag = dot_f32(left, other, NT)
            packed = jnp.where(rows <= cols, real, imag)
            vis_ref[v] = (packed * gain_col * gain_row).astype(jnp.bfloat16)
            copies.append(pltpu.make_async_copy(vis_ref.at[v], vis_hbm.at[v], out_sem.at[v]))
            copies[v].start()
        for copy in copies:
            copy.wait()
        zero.wait()

    @pl.when(is_beam)
    def _():
        vis_ref[...] = jnp.zeros_like(vis_ref)
        zero = pltpu.make_async_copy(vis_ref, vis_hbm, zero_sem)
        zero.start()
        gain = None
        for j in range(VIS_LOCAL, -1, -1):
            part = dot_f32(split_ref[...], r_ref[j], NN)
            if gain is None:
                gain = jnp.sum(part[:, GAIN_LANE : GAIN_LANE + 3], axis=1, keepdims=True)
            xs_ref[j] = (part * gain).astype(jnp.bfloat16)
        q_row = lax.broadcasted_iota(jnp.int32, (BLOCK, INPUTS), 0)
        q_col = lax.broadcasted_iota(jnp.int32, (BLOCK, INPUTS), 1)
        scale = 1.0 / math.sqrt(STATIONS)
        copies = []
        for v in range(VIS_LOCAL):
            window = jnp.concatenate([xs_ref[v], xs_ref[v + 1]], axis=1)
            keep = jnp.where(q_col == q_row + 16 * v, 1.0, 0.0).astype(jnp.bfloat16)
            plain = dot_f32(keep, window, NT)
            other = dot_f32(swap_ref[v, 16 * v : 16 * v + BLOCK, :], window, NT)
            for pol in range(POLS):
                rows = pl.ds(2 * BLOCK * v + pol, BLOCK, stride=2)
                half = slice(128 * pol, 128 * pol + 128)
                xl_ref[0, rows, :] = plain[:, half]
                xl_ref[1, rows, :] = other[:, half]
            for k in range(AVG * v, AVG * v + AVG):
                rows = slice(24 * k, 24 * k + 24)
                left = jnp.concatenate([xl_ref[0, rows, :], xl_ref[1, rows, :]], axis=1)
                out = dot_f32(left.astype(jnp.bfloat16), w_ref[k], NN) * scale
                beam_ref[k] = out.astype(jnp.bfloat16).reshape(2 * FRAMES, POLS, BEAMS)
            part = pl.ds(AVG * v, AVG)
            copies.append(
                pltpu.make_async_copy(beam_ref.at[part], beam_hbm.at[part], out_sem.at[v])
            )
            copies[v].start()
        for copy in copies:
            copy.wait()
        zero.wait()


def finish(section, weights, received, swap, split):
    vmem = pl.BlockSpec(memory_space=pltpu.VMEM)
    anywhere = pl.BlockSpec(memory_space=pl.ANY)
    vis_shape = (VIS_LOCAL, INPUTS, INPUTS)
    beam_shape = (PER_GROUP, 2 * FRAMES, POLS, BEAMS)
    vis, beam = pl.pallas_call(
        finish_kernel,
        out_shape=(
            jax.ShapeDtypeStruct(vis_shape, jnp.bfloat16),
            jax.ShapeDtypeStruct(beam_shape, jnp.bfloat16),
        ),
        in_specs=[vmem] * 5,
        out_specs=(anywhere, anywhere),
        scratch_shapes=[
            pltpu.VMEM(vis_shape, jnp.bfloat16),
            pltpu.VMEM(beam_shape, jnp.bfloat16),
            pltpu.VMEM((2, PER_GROUP * 24, 128), jnp.float32),
            pltpu.VMEM((5, INPUTS, 128), jnp.bfloat16),
            pltpu.SemaphoreType.DMA((4,)),
            pltpu.SemaphoreType.DMA,
        ],
        compiler_params=pltpu.CompilerParams(vmem_limit_bytes=24 << 20),
        name="finish",
    )(section, weights, received, swap, split)
    tied = beam.reshape(PER_GROUP, 2, FRAMES, POLS, BEAMS).transpose(0, 1, 3, 2, 4)
    return vis, tied


def split2(value):
    high = value.astype(jnp.bfloat16)
    return high, (value - high.astype(jnp.float32)).astype(jnp.bfloat16)


def split_const(table):
    table = np.asarray(table, np.float32)
    high = table.astype(jnp.bfloat16)
    return high, (table - high.astype(np.float32)).astype(jnp.bfloat16)


def taper_table():
    index = np.arange(TAPS * NCH, dtype=np.float64)
    offset = (index + 0.5 - TAPS * NCH / 2.0) / NCH
    window = 0.5 - 0.5 * np.cos(2.0 * np.pi * (index + 0.5) / (TAPS * NCH))
    table = (np.sinc(offset) * window).reshape(TAPS, PER_GROUP, 1, 128)
    table = np.broadcast_to(table, (TAPS, PER_GROUP, POLS, 128))
    return table.reshape(TAPS, 2 * PER_GROUP, 128).astype(np.float32)


def outer_table():
    angle = 2.0 * np.pi * (np.outer(np.arange(48), np.arange(48)) % 48) / 48.0
    cos, sin = np.cos(angle), np.sin(angle)
    table = np.zeros((POLS, 2, 48, 2, 48, POLS))
    for pol in range(POLS):
        table[pol, 0, :, 0, :, pol] = cos
        table[pol, 0, :, 1, :, pol] = sin
        table[pol, 1, :, 0, :, pol] = -sin
        table[pol, 1, :, 1, :, pol] = cos
    return table.reshape(192, 192)


def twist_tables():
    angle = 2.0 * np.pi * np.outer(np.arange(48), np.arange(128)) / NCH
    return np.stack([np.cos(angle), np.sin(angle)]).astype(np.float32)


def inner_table():
    angle = 2.0 * np.pi * (np.outer(np.arange(128), np.arange(128)) % 128) / 128.0
    return np.concatenate([np.cos(angle), np.sin(angle)], axis=1)


def spread_table():
    row, col = np.arange(384)[:, None], np.arange(640)[None, :]
    return ((row % 48 == col // 12) & (col < 576)).astype(np.float32)


def make_weights(delays, first, w_ref):
    delay = delays.astype(jnp.float32).T.astype(jnp.int32)
    turn = 2.0 * math.pi / PERIOD
    start = (delay * first & (PERIOD - 1)).astype(jnp.float32) * turn
    step = delay.astype(jnp.float32) * turn
    state = (jnp.cos(start), jnp.sin(start), jnp.cos(step), jnp.sin(step))
    for sb in range(8):
        cs, sn, dc, ds = (t[16 * sb : 16 * sb + 16] for t in state)

        def advance(k, carry):
            c, s = carry
            w_ref[k, 16 * sb : 16 * sb + 16, :] = c.astype(jnp.bfloat16)
            w_ref[k, 128 + 16 * sb : 128 + 16 * sb + 16, :] = s.astype(jnp.bfloat16)
            return (c * dc - s * ds, c * ds + s * dc)

        lax.fori_loop(0, PER_GROUP, advance, (cs, sn), unroll=4)


def channelize_kernel(
    flag_ref,
    volt_hbm,
    band_hbm,
    delays_hbm,
    taper_hbm,
    outer_hbm,
    twist_hbm,
    inner_hbm,
    spread_hbm,
    section_hbm,
    swap_hbm,
    split_hbm,
    recv_ref,
    w_ref,
    section_ref,
    swap_ref,
    split_ref,
    volt_ref,
    band_ref,
    delays_ref,
    taper_ref,
    outer_ref,
    twist_ref,
    inner_ref,
    spread_ref,
    choice_ref,
    f_ref,
    y_ref,
    o_ref,
    send_ref,
    pow_ref,
    load_sem,
    send_sem,
    recv_sem,
    own_sem,
    ready_sem,
    high_sem,
    all_sem,
):
    me, sec = lax.axis_index("stn"), lax.axis_index("sec")
    plane, place = me // PLANE, lax.rem(me, PLANE)
    barrier = pltpu.get_barrier_semaphore()
    loads = [
        pltpu.make_async_copy(src, dst, load_sem.at[n])
        for n, (src, dst) in enumerate(
            (
                (taper_hbm, taper_ref),
                (volt_hbm.at[0], volt_ref.at[0]),
                (volt_hbm.at[1], volt_ref.at[1]),
                (band_hbm, band_ref),
                (spread_hbm, spread_ref),
                (outer_hbm, outer_ref),
                (twist_hbm, twist_ref),
                (inner_hbm, inner_ref),
                (delays_hbm, delays_ref),
                (section_hbm, choice_ref),
                (swap_hbm, swap_ref),
                (split_hbm, split_ref),
            )
        )
    ]
    for load in loads:
        load.start()

    is_low = plane < HALF

    @pl.when(is_low)
    def _():
        for i in range(1, PLANE):
            other = plane * PLANE + lax.rem(place + i, PLANE)
            pl.semaphore_signal(barrier, inc=1, device_id=(other, sec), device_id_type=MESH)

    for i in range(1, SECTIONS):
        other = lax.rem(sec + i, SECTIONS)
        pl.semaphore_signal(barrier, inc=1, device_id=(me, other), device_id_type=MESH)
    loads[0].wait()
    for part in range(2):
        loads[1 + part].wait()
        if part == 1:
            for load in loads[3:8]:
                load.wait()
        for chunk in range(6):
            rows = slice(16 * chunk, 16 * chunk + 16)
            taps = [taper_ref[j, rows, :] for j in range(TAPS)]
            blocks = [
                volt_ref[part, 96 * n + 16 * chunk : 96 * n + 16 * chunk + 16, :].astype(jnp.float32)
                for n in range(FRAMES + TAPS - 1)
            ]
            at = 96 * part + 16 * chunk
            for m in range(FRAMES):
                total = taps[0] * blocks[m]
                for j in range(1, TAPS):
                    total = total + taps[j] * blocks[m + j]
                high, low = split2(total)
                lanes = slice(128 * m, 128 * m + 128)
                f_ref[at : at + 16, lanes] = high
                f_ref[192 + at : 192 + at + 16, lanes] = high
                f_ref[384 + at : 384 + at + 16, lanes] = low

    group = lax.broadcasted_iota(jnp.int32, (8, 128), 0)
    lane8 = lax.broadcasted_iota(jnp.int32, (8, 128), 1)
    spread_parts = []
    for q in range(3):
        inside = (lane8 + 128 * q >= 48 * group) & (lane8 + 128 * q < 48 * group + 48)
        tiles = [
            jnp.where(inside, band_ref[0:1, 384 * t + 128 * q : 384 * t + 128 * q + 128], 0.0)
            for t in range(16)
        ]
        spread_parts.append(jnp.concatenate(tiles, axis=0))
    band_h, band_l = split2(jnp.concatenate(spread_parts, axis=1))

    cos, sin = twist_ref[0], twist_ref[1]
    for pair in range(FRAMES // 2):
        lanes = slice(256 * pair, 256 * pair + 256)
        seg = dot_f32(outer_ref[...], f_ref[:, lanes], NN)
        for half in range(2):
            m = 2 * pair + half
            for pol in range(POLS):
                sr = seg[96 * pol : 96 * pol + 48, 128 * half : 128 * half + 128]
                si = seg[96 * pol + 48 : 96 * pol + 96, 128 * half : 128 * half + 128]
                yr = sr * cos + si * sin
                yi = si * cos - sr * sin
                real_rows = pl.ds(m, 48, stride=12)
                imag_rows = pl.ds(FRAMES + m, 48, stride=12)
                y_ref[2 * pol, real_rows, :] = yr
                y_ref[2 * pol + 1, real_rows, :] = yi
                y_ref[2 * pol, imag_rows, :] = yi
                y_ref[2 * pol + 1, imag_rows, :] = -yr

    powers = [jnp.zeros((8, 128), jnp.float32) for _ in range(POLS)]
    for first, count in ((0, 2), (2, 2), (4, 1)):
        width = 128 * count
        depth = min(width, 576 - 128 * first)
        columns = spread_ref[:, 128 * first : 128 * first + width]
        spread = dot_f32(band_h, columns, NN) + dot_f32(band_l, columns, NN)
        for pol in range(POLS):
            y = jnp.concatenate(
                [y_ref[2 * pol + t, 128 * first : 128 * first + depth, :] for t in range(2)], axis=1
            )
            if depth < width:
                y = jnp.concatenate([y, jnp.zeros((width - depth, 256), jnp.float32)], axis=0)
            yh, yl = split2(y)
            out = dot_f32(inner_ref[...], jnp.concatenate([yh, yh, yl], axis=1), NT)
            out = out * spread
            square = out * out
            for t in range(count):
                piece = slice(128 * t, 128 * t + 128)
                o_ref[first + t, pl.ds(pol, 128, stride=2), :] = out[:, piece]
                powers[pol] = powers[pol] + jnp.sum(square[:, piece].reshape(16, 8, 128), axis=0)
    lane = lax.broadcasted_iota(jnp.int32, (1, 128), 1)
    totals = [jnp.sum(p, keepdims=True) for p in powers]
    pow_ref[SECTIONS] = jnp.where(lane < 64, totals[0], totals[1])

    def at_place(z):
        return (z * PLANE + place, sec)

    @pl.when(is_low)
    def _():
        pl.semaphore_wait(barrier, PLANE - 1 + SECTIONS - 1 + plane)

        def greet_later(z, carry):
            pl.semaphore_signal(barrier, inc=1, device_id=at_place(z), device_id_type=MESH)
            return carry

        def greet_earlier(z, carry):
            pl.semaphore_signal(
                ready_sem.at[plane], inc=1, device_id=at_place(z), device_id_type=MESH
            )
            return carry

        lax.fori_loop(plane + 1, PLANES, greet_later, 0)
        lax.fori_loop(0, plane, greet_earlier, 0)

    @pl.when(jnp.logical_not(is_low))
    def _():
        pl.semaphore_wait(barrier, SECTIONS - 1 + HALF)

    def power_copy(j):
        return pltpu.make_async_remote_copy(
            src_ref=pow_ref.at[SECTIONS],
            dst_ref=pow_ref.at[sec],
            send_sem=send_sem.at[0],
            recv_sem=recv_sem.at[0],
            device_id=(me, lax.rem(sec + j, SECTIONS)),
            device_id_type=MESH,
        )

    for j in range(1, SECTIONS):
        power_copy(j).start()
    for j in range(4):
        send_ref[j] = o_ref[j].astype(jnp.bfloat16).reshape(128, 2, 128)

    def block_copy(to, tiles):
        return pltpu.make_async_remote_copy(
            src_ref=send_ref.at[tiles, to],
            dst_ref=recv_ref.at[tiles, me],
            send_sem=send_sem.at[1],
            recv_sem=recv_sem.at[1],
            device_id=(to, sec),
            device_id_type=MESH,
        )

    body, tail, whole = pl.ds(0, 4), pl.ds(4, 1), pl.ds(0, 5)

    def send_plane(z, tiles, mates=False):
        for i in PLACES[: PLANE - 1] if mates else PLACES:
            block_copy(z * PLANE + lax.rem(place + i, PLANE), tiles).start()

    def send_low_half(tiles, first):
        def one(n, carry):
            send_plane(lax.rem(first + n, HALF), tiles)
            return carry

        lax.fori_loop(0, HALF, one, 0)

    @pl.when(jnp.logical_not(is_low))
    def _():
        mirror = PLANES - 1 - plane
        for i in PLACES:
            other = mirror * PLANE + lax.rem(place + i, PLANE)
            pl.semaphore_signal(high_sem, inc=1, device_id=(other, sec), device_id_type=MESH)
        send_low_half(body, plane)

    def bytes_of(ref, slot):
        return pltpu.make_async_remote_copy(
            src_ref=ref,
            dst_ref=ref,
            send_sem=send_sem.at[slot],
            recv_sem=recv_sem.at[slot],
            device_id=(me, sec),
            device_id_type=MESH,
        )

    three = bytes_of(pow_ref.at[pl.ds(0, SECTIONS - 1)], 0)
    three.wait_send()
    three.wait_recv()
    mine = lax.broadcasted_iota(jnp.int32, (1, 128), 1) * 0 + sec
    total = pow_ref[SECTIONS]
    for other in range(SECTIONS):
        total = total + jnp.where(mine == other, 0.0, pow_ref[other])
    mean = total * (1.0 / (SECTIONS * FRAMES * NCH))
    gain = jnp.where(flag_ref[0] == 1, 0.0, 1.0 / jnp.sqrt(mean + 1e-05))
    g0 = gain.astype(jnp.bfloat16).astype(jnp.float32)
    g1 = (gain - g0).astype(jnp.bfloat16).astype(jnp.float32)
    g2 = gain - g0 - g1
    row = lax.broadcasted_iota(jnp.int32, (8, 128), 0)
    col = lax.broadcasted_iota(jnp.int32, (8, 128), 1)
    patch = jnp.zeros((8, 128), jnp.float32)
    for at, g in ((0, g0), (1, g1), (2, g2)):
        pair = jnp.where(row % 2 == 0, g[:, 0:1], g[:, 64:65])
        patch = jnp.where(col == GAIN_LANE + at, pair, patch)
    patch = jnp.broadcast_to(patch[None], (INPUTS // 8, 8, 128)).reshape(INPUTS, 128)
    wide = lax.broadcasted_iota(jnp.int32, (INPUTS, 128), 1)
    tile = jnp.where(wide < GAIN_LANE, o_ref[4], patch)
    send_ref[4] = tile.astype(jnp.bfloat16).reshape(128, 2, 128)
    def send_ready(z):
        pl.semaphore_wait(ready_sem.at[z], 1)
        send_plane(z, whole)

    @pl.when(is_low)
    def _():
        def earlier(z, carry):
            send_plane(z, whole)
            return carry

        def later(z, carry):
            send_ready(z)
            return carry

        send_plane(plane, whole, mates=True)
        lax.fori_loop(0, plane, earlier, 0)
        lax.fori_loop(plane + 1, HALF, later, 0)

    @pl.when(jnp.logical_not(is_low))
    def _():
        send_low_half(tail, 0)

    own = pltpu.make_async_copy(send_ref.at[:, me], recv_ref.at[:, me], own_sem)
    own.start()
    for load in loads[8:]:
        load.wait()
    section_ref[...] = jnp.full((8, 128), choice_ref[sec]).astype(jnp.float32)
    make_weights(delays_ref[...], sec * NCH + me * PER_GROUP, w_ref)

    @pl.when(is_low)
    def _():
        mirror = PLANES - 1 - plane
        pl.semaphore_wait(high_sem, PLANE)
        for i in range(1, HALF):
            other = lax.rem(plane + i, HALF)
            pl.semaphore_signal(
                ready_sem.at[mirror], inc=1, device_id=at_place(other), device_id_type=MESH
            )
        send_plane(mirror, whole)

        def other_high(n, carry):
            send_ready(HALF + lax.rem(mirror + n, HALF))
            return carry

        lax.fori_loop(1, HALF - 1, other_high, 0)
        last = HALF + lax.rem(mirror + HALF - 1, HALF)
        pl.semaphore_wait(ready_sem.at[last], 1)
        pl.semaphore_signal(all_sem, inc=1, device_id=at_place(mirror), device_id_type=MESH)
        send_plane(last, whole)

    @pl.when(jnp.logical_not(is_low))
    def _():
        pl.semaphore_wait(all_sem, 1)
        send_plane(plane, whole, mates=True)

        def mates(n, carry):
            send_plane(HALF + lax.rem(plane + n, HALF), whole)
            return carry

        lax.fori_loop(1, HALF, mates, 0)

    own.wait()
    sent = bytes_of(send_ref.at[:, pl.ds(0, STATIONS - 1)], 1)
    sent.wait_send()
    landed = bytes_of(recv_ref.at[:, pl.ds(0, STATIONS - 1)], 1)
    landed.wait_recv()


def channelize(volts, band, delays, flags, section):
    outer_h, outer_l = split_const(outer_table())
    inner_h, inner_l = split_const(inner_table())
    inputs = [
        volts,
        band,
        delays,
        jnp.asarray(taper_table()),
        jnp.asarray(np.concatenate([outer_h, outer_l, outer_h], axis=1)),
        jnp.asarray(twist_tables()),
        jnp.asarray(np.concatenate([inner_h, inner_l, inner_h], axis=1)),
        jnp.asarray(spread_table(), jnp.bfloat16),
    ]
    swap = jnp.asarray(swap_table(), jnp.bfloat16)
    split = jnp.asarray(split_table(), jnp.bfloat16)
    operands = [
        pltpu.with_memory_space_constraint(x, pltpu.HBM)
        for x in inputs + [section, swap, split]
    ]
    vmem = pl.BlockSpec(memory_space=pltpu.VMEM)
    return pl.pallas_call(
        channelize_kernel,
        out_shape=(
            pltpu.VMEM((5, STATIONS, POLS, 128), jnp.bfloat16),
            pltpu.VMEM((PER_GROUP, INPUTS, BEAMS), jnp.bfloat16),
            pltpu.VMEM((8, 128), jnp.float32),
            pltpu.VMEM(swap.shape, swap.dtype),
            pltpu.VMEM(split.shape, split.dtype),
        ),
        in_specs=[pl.BlockSpec(memory_space=pltpu.SMEM)]
        + [pl.BlockSpec(memory_space=pltpu.HBM)] * len(operands),
        out_specs=(vmem,) * 5,
        scratch_shapes=[pltpu.VMEM(x.shape, x.dtype) for x in inputs]
        + [
            pltpu.SMEM(section.shape, section.dtype),
            pltpu.VMEM((576, 768), jnp.bfloat16),
            pltpu.VMEM((4, 576, 128), jnp.float32),
            pltpu.VMEM((5, 256, 128), jnp.float32),
            pltpu.VMEM((5, STATIONS, POLS, 128), jnp.bfloat16),
            pltpu.VMEM((5, 1, 128), jnp.float32),
            pltpu.SemaphoreType.DMA((len(operands) + 1,)),
            pltpu.SemaphoreType.DMA((2,)),
            pltpu.SemaphoreType.DMA((2,)),
            pltpu.SemaphoreType.DMA,
            pltpu.SemaphoreType.REGULAR((PLANES,)),
            pltpu.SemaphoreType.REGULAR,
            pltpu.SemaphoreType.REGULAR,
        ],
        compiler_params=pltpu.CompilerParams(
            collective_id=0, has_side_effects=True, vmem_limit_bytes=24 << 20
        ),
        name="channelize",
    )(flags, *operands)


def per_device(voltages, bandpass, station_flags, delays, section):
    volts = voltages.reshape(2, POLS, 624, 128).transpose(0, 2, 1, 3).reshape(2, 1248, 128)
    turned, weights, choice, swap, split = channelize(
        volts, bandpass, delays, station_flags, section
    )
    vis, tied = finish(choice, weights, turned.reshape(5, INPUTS, 128), swap, split)
    return (vis[None], tied[None])


def solution(mesh):
    return jax.shard_map(
        per_device,
        mesh=mesh,
        in_specs=(P(None, "stn", "sec", None, None), P("sec", None), P("stn"), P(), P()),
        out_specs=(P("sec", "stn", None, None), P("sec", "stn", None, None, None, None)),
        check_vma=False,
    )
```

```python
import functools
import math

import jax
import jax.numpy as jnp
import numpy as np
from jax import lax
from jax.experimental import pallas as pl
from jax.experimental.pallas import tpu as pltpu
from jax.sharding import PartitionSpec as P

POLS = 2
NCH = 6144
TAPS = 8
FRAMES = 6
AVG = 12
BEAMS = 256
STATIONS = 128
INPUTS = STATIONS * POLS
PER_GROUP = 48
VIS_LOCAL = PER_GROUP // AVG
BLOCK = AVG * 2 * FRAMES
PERIOD = 65536
GAIN_LANE = 64
PLANES = 8
PLANE = STATIONS // PLANES
SECTIONS = 4
HALF = PLANES // 2
PLACES = (8, 9, 6, 7, 10, 11, 4, 5, 12, 13, 2, 3, 14, 15, 1, 0)
MESH = pl.DeviceIdType.MESH

NT = (((1,), (1,)), ((), ()))
NN = (((1,), (0,)), ((), ()))


def dot_f32(lhs, rhs, dims):
    return lax.dot_general(lhs, rhs, dims, preferred_element_type=jnp.float32)


def swap_table():
    table = np.zeros((VIS_LOCAL, INPUTS, INPUTS), np.float32)
    for v in range(VIS_LOCAL):
        for q in range(BLOCK):
            real = q % 12 < 6
            table[v, 16 * v + q, 16 * v + (q + 6 if real else q - 6)] = -1.0 if real else 1.0
    return table


def split_table():
    table = np.zeros((INPUTS, INPUTS), np.float32)
    for pol in range(POLS):
        for station in range(STATIONS):
            table[pol * STATIONS + station, station * POLS + pol] = 1.0
    return table


def finish_kernel(
    section_ref,
    w_ref,
    r_ref,
    swap_ref,
    split_ref,
    vis_hbm,
    beam_hbm,
    vis_ref,
    beam_ref,
    xl_ref,
    xs_ref,
    out_sem,
    zero_sem,
):
    is_beam = jnp.max(section_ref[...]) == 1.0

    @pl.when(jnp.logical_not(is_beam))
    def _():
        beam_ref[...] = jnp.zeros_like(beam_ref)
        zero = pltpu.make_async_copy(beam_ref, beam_hbm, zero_sem)
        zero.start()
        copies = []
        last = r_ref[VIS_LOCAL]
        gain_col = jnp.sum(
            last[:, GAIN_LANE : GAIN_LANE + 3].astype(jnp.float32), axis=1, keepdims=True
        )
        gain_col = gain_col * (1.0 / math.sqrt(FRAMES * AVG))
        lane8 = lax.broadcasted_iota(jnp.int32, (8, 128), 1)
        pick = jnp.where((lane8 >= GAIN_LANE) & (lane8 < GAIN_LANE + 3), 1.0, 0.0)
        gain_row = dot_f32(pick.astype(jnp.bfloat16), last, NT)[0:1, :]
        rows = lax.broadcasted_iota(jnp.int32, (INPUTS, INPUTS), 0)
        cols = lax.broadcasted_iota(jnp.int32, (INPUTS, INPUTS), 1)
        for v in range(VIS_LOCAL):
            left = jnp.concatenate([r_ref[v], r_ref[v + 1]], axis=1)
            inside = (cols >= 16 * v) & (cols < 16 * v + BLOCK)
            same = jnp.where(inside, left.astype(jnp.float32), 0.0).astype(jnp.bfloat16)
            other = dot_f32(left, swap_ref[v], NT).astype(jnp.bfloat16)
            real = dot_f32(left, same, NT)
            imag = dot_f32(left, other, NT)
            packed = jnp.where(rows <= cols, real, imag)
            vis_ref[v] = (packed * gain_col * gain_row).astype(jnp.bfloat16)
            copies.append(pltpu.make_async_copy(vis_ref.at[v], vis_hbm.at[v], out_sem.at[v]))
            copies[v].start()
        for copy in copies:
            copy.wait()
        zero.wait()

    @pl.when(is_beam)
    def _():
        vis_ref[...] = jnp.zeros_like(vis_ref)
        zero = pltpu.make_async_copy(vis_ref, vis_hbm, zero_sem)
        zero.start()
        gain = None
        for j in range(VIS_LOCAL, -1, -1):
            part = dot_f32(split_ref[...], r_ref[j], NN)
            if gain is None:
                gain = jnp.sum(part[:, GAIN_LANE : GAIN_LANE + 3], axis=1, keepdims=True)
            xs_ref[j] = (part * gain).astype(jnp.bfloat16)
        q_row = lax.broadcasted_iota(jnp.int32, (BLOCK, INPUTS), 0)
        q_col = lax.broadcasted_iota(jnp.int32, (BLOCK, INPUTS), 1)
        scale = 1.0 / math.sqrt(STATIONS)
        copies = []
        for v in range(VIS_LOCAL):
            window = jnp.concatenate([xs_ref[v], xs_ref[v + 1]], axis=1)
            keep = jnp.where(q_col == q_row + 16 * v, 1.0, 0.0).astype(jnp.bfloat16)
            plain = dot_f32(keep, window, NT)
            other = dot_f32(swap_ref[v, 16 * v : 16 * v + BLOCK, :], window, NT)
            for pol in range(POLS):
                rows = pl.ds(2 * BLOCK * v + pol, BLOCK, stride=2)
                half = slice(128 * pol, 128 * pol + 128)
                xl_ref[0, rows, :] = plain[:, half]
                xl_ref[1, rows, :] = other[:, half]
            for k in range(AVG * v, AVG * v + AVG):
                rows = slice(24 * k, 24 * k + 24)
                left = jnp.concatenate([xl_ref[0, rows, :], xl_ref[1, rows, :]], axis=1)
                out = dot_f32(left.astype(jnp.bfloat16), w_ref[k], NN) * scale
                beam_ref[k] = out.astype(jnp.bfloat16).reshape(2 * FRAMES, POLS, BEAMS)
            part = pl.ds(AVG * v, AVG)
            copies.append(
                pltpu.make_async_copy(beam_ref.at[part], beam_hbm.at[part], out_sem.at[v])
            )
            copies[v].start()
        for copy in copies:
            copy.wait()
        zero.wait()


def finish(section, weights, received, swap, split):
    vmem = pl.BlockSpec(memory_space=pltpu.VMEM)
    anywhere = pl.BlockSpec(memory_space=pl.ANY)
    vis_shape = (VIS_LOCAL, INPUTS, INPUTS)
    beam_shape = (PER_GROUP, 2 * FRAMES, POLS, BEAMS)
    vis, beam = pl.pallas_call(
        finish_kernel,
        out_shape=(
            jax.ShapeDtypeStruct(vis_shape, jnp.bfloat16),
            jax.ShapeDtypeStruct(beam_shape, jnp.bfloat16),
        ),
        in_specs=[vmem] * 5,
        out_specs=(anywhere, anywhere),
        scratch_shapes=[
            pltpu.VMEM(vis_shape, jnp.bfloat16),
            pltpu.VMEM(beam_shape, jnp.bfloat16),
            pltpu.VMEM((2, PER_GROUP * 24, 128), jnp.float32),
            pltpu.VMEM((5, INPUTS, 128), jnp.bfloat16),
            pltpu.SemaphoreType.DMA((4,)),
            pltpu.SemaphoreType.DMA,
        ],
        compiler_params=pltpu.CompilerParams(vmem_limit_bytes=24 << 20),
        name="finish",
    )(section, weights, received, swap, split)
    tied = beam.reshape(PER_GROUP, 2, FRAMES, POLS, BEAMS).transpose(0, 1, 3, 2, 4)
    return vis, tied


def split2(value):
    high = value.astype(jnp.bfloat16)
    return high, (value - high.astype(jnp.float32)).astype(jnp.bfloat16)


def split_const(table):
    table = np.asarray(table, np.float32)
    high = table.astype(jnp.bfloat16)
    return high, (table - high.astype(np.float32)).astype(jnp.bfloat16)


def taper_table():
    index = np.arange(TAPS * NCH, dtype=np.float64)
    offset = (index + 0.5 - TAPS * NCH / 2.0) / NCH
    window = 0.5 - 0.5 * np.cos(2.0 * np.pi * (index + 0.5) / (TAPS * NCH))
    table = (np.sinc(offset) * window).reshape(TAPS, PER_GROUP, 1, 128)
    table = np.broadcast_to(table, (TAPS, PER_GROUP, POLS, 128))
    return table.reshape(TAPS, 2 * PER_GROUP, 128).astype(np.float32)


def outer_table():
    angle = 2.0 * np.pi * (np.outer(np.arange(48), np.arange(48)) % 48) / 48.0
    cos, sin = np.cos(angle), np.sin(angle)
    table = np.zeros((POLS, 2, 48, 2, 48, POLS))
    for pol in range(POLS):
        table[pol, 0, :, 0, :, pol] = cos
        table[pol, 0, :, 1, :, pol] = sin
        table[pol, 1, :, 0, :, pol] = -sin
        table[pol, 1, :, 1, :, pol] = cos
    return table.reshape(192, 192)


def twist_tables():
    angle = 2.0 * np.pi * np.outer(np.arange(48), np.arange(128)) / NCH
    return np.stack([np.cos(angle), np.sin(angle)]).astype(np.float32)


def inner_table():
    angle = 2.0 * np.pi * (np.outer(np.arange(128), np.arange(128)) % 128) / 128.0
    return np.concatenate([np.cos(angle), np.sin(angle)], axis=1)


def spread_table():
    row, col = np.arange(384)[:, None], np.arange(640)[None, :]
    return ((row % 48 == col // 12) & (col < 576)).astype(np.float32)


def make_weights(delays, first, w_ref):
    delay = delays.astype(jnp.float32).T.astype(jnp.int32)
    turn = 2.0 * math.pi / PERIOD
    start = (delay * first & (PERIOD - 1)).astype(jnp.float32) * turn
    step = delay.astype(jnp.float32) * turn
    state = (jnp.cos(start), jnp.sin(start), jnp.cos(step), jnp.sin(step))
    for sb in range(8):
        cs, sn, dc, ds = (t[16 * sb : 16 * sb + 16] for t in state)

        def advance(k, carry):
            c, s = carry
            w_ref[k, 16 * sb : 16 * sb + 16, :] = c.astype(jnp.bfloat16)
            w_ref[k, 128 + 16 * sb : 128 + 16 * sb + 16, :] = s.astype(jnp.bfloat16)
            return (c * dc - s * ds, c * ds + s * dc)

        lax.fori_loop(0, PER_GROUP, advance, (cs, sn), unroll=4)


def channelize_kernel(
    flag_ref,
    volt_hbm,
    band_hbm,
    delays_hbm,
    taper_hbm,
    outer_hbm,
    twist_hbm,
    inner_hbm,
    spread_hbm,
    section_hbm,
    swap_hbm,
    split_hbm,
    recv_ref,
    w_ref,
    section_ref,
    swap_ref,
    split_ref,
    volt_ref,
    band_ref,
    delays_ref,
    taper_ref,
    outer_ref,
    twist_ref,
    inner_ref,
    spread_ref,
    choice_ref,
    f_ref,
    y_ref,
    o_ref,
    send_ref,
    pow_ref,
    load_sem,
    send_sem,
    recv_sem,
    own_sem,
    ready_sem,
    high_sem,
    all_sem,
):
    me, sec = lax.axis_index("stn"), lax.axis_index("sec")
    plane, place = me // PLANE, lax.rem(me, PLANE)
    barrier = pltpu.get_barrier_semaphore()
    loads = [
        pltpu.make_async_copy(src, dst, load_sem.at[n])
        for n, (src, dst) in enumerate(
            (
                (taper_hbm, taper_ref),
                (volt_hbm.at[0], volt_ref.at[0]),
                (volt_hbm.at[1], volt_ref.at[1]),
                (band_hbm, band_ref),
                (spread_hbm, spread_ref),
                (outer_hbm, outer_ref),
                (twist_hbm, twist_ref),
                (inner_hbm, inner_ref),
                (delays_hbm, delays_ref),
                (section_hbm, choice_ref),
                (swap_hbm, swap_ref),
                (split_hbm, split_ref),
            )
        )
    ]
    for load in loads:
        load.start()

    is_low = plane < HALF

    @pl.when(is_low)
    def _():
        for i in range(1, PLANE):
            other = plane * PLANE + lax.rem(place + i, PLANE)
            pl.semaphore_signal(barrier, inc=1, device_id=(other, sec), device_id_type=MESH)

    for i in range(1, SECTIONS):
        other = lax.rem(sec + i, SECTIONS)
        pl.semaphore_signal(barrier, inc=1, device_id=(me, other), device_id_type=MESH)
    loads[0].wait()
    for part in range(2):
        loads[1 + part].wait()
        if part == 1:
            for load in loads[3:8]:
                load.wait()
        for chunk in range(6):
            rows = slice(16 * chunk, 16 * chunk + 16)
            taps = [taper_ref[j, rows, :] for j in range(TAPS)]
            blocks = [
                volt_ref[part, 96 * n + 16 * chunk : 96 * n + 16 * chunk + 16, :].astype(jnp.float32)
                for n in range(FRAMES + TAPS - 1)
            ]
            at = 96 * part + 16 * chunk
            for m in range(FRAMES):
                total = taps[0] * blocks[m]
                for j in range(1, TAPS):
                    total = total + taps[j] * blocks[m + j]
                high, low = split2(total)
                lanes = slice(128 * m, 128 * m + 128)
                f_ref[at : at + 16, lanes] = high
                f_ref[192 + at : 192 + at + 16, lanes] = low

    group = lax.broadcasted_iota(jnp.int32, (8, 128), 0)
    lane8 = lax.broadcasted_iota(jnp.int32, (8, 128), 1)
    spread_parts = []
    for q in range(3):
        inside = (lane8 + 128 * q >= 48 * group) & (lane8 + 128 * q < 48 * group + 48)
        tiles = [
            jnp.where(inside, band_ref[0:1, 384 * t + 128 * q : 384 * t + 128 * q + 128], 0.0)
            for t in range(16)
        ]
        spread_parts.append(jnp.concatenate(tiles, axis=0))
    bands = jnp.concatenate(split2(jnp.concatenate(spread_parts, axis=1)), axis=0)

    cos, sin = twist_ref[0], twist_ref[1]
    for pair in range(FRAMES // 2):
        lanes = slice(256 * pair, 256 * pair + 256)
        both = dot_f32(outer_ref[...], f_ref[0:192, lanes], NN)
        seg = both[:192] + both[192:] + dot_f32(outer_ref[0:192, :], f_ref[192:384, lanes], NN)
        for half in range(2):
            m = 2 * pair + half
            for pol in range(POLS):
                sr = seg[96 * pol : 96 * pol + 48, 128 * half : 128 * half + 128]
                si = seg[96 * pol + 48 : 96 * pol + 96, 128 * half : 128 * half + 128]
                yr = sr * cos + si * sin
                yi = si * cos - sr * sin
                real_rows = pl.ds(m, 48, stride=12)
                imag_rows = pl.ds(FRAMES + m, 48, stride=12)
                y_ref[2 * pol, real_rows, :] = yr
                y_ref[2 * pol + 1, real_rows, :] = yi
                y_ref[2 * pol, imag_rows, :] = yi
                y_ref[2 * pol + 1, imag_rows, :] = -yr

    powers = [jnp.zeros((8, 128), jnp.float32) for _ in range(POLS)]
    for first, count in ((0, 2), (2, 2), (4, 1)):
        width = 128 * count
        depth = min(width, 576 - 128 * first)
        columns = spread_ref[:, 128 * first : 128 * first + width]
        spread = dot_f32(bands, columns, NN)
        spread = spread[:128] + spread[128:]
        for pol in range(POLS):
            y = jnp.concatenate(
                [y_ref[2 * pol + t, 128 * first : 128 * first + depth, :] for t in range(2)], axis=1
            )
            if depth < width:
                y = jnp.concatenate([y, jnp.zeros((width - depth, 256), jnp.float32)], axis=0)
            yh, yl = split2(y)
            both = dot_f32(inner_ref[...], yh, NT)
            out = both[:128] + both[128:] + dot_f32(inner_ref[0:128, :], yl, NT)
            out = out * spread
            square = out * out
            for t in range(count):
                piece = slice(128 * t, 128 * t + 128)
                o_ref[first + t, pl.ds(pol, 128, stride=2), :] = out[:, piece]
                powers[pol] = powers[pol] + jnp.sum(square[:, piece].reshape(16, 8, 128), axis=0)
    lane = lax.broadcasted_iota(jnp.int32, (1, 128), 1)
    totals = [jnp.sum(p, keepdims=True) for p in powers]
    pow_ref[SECTIONS] = jnp.where(lane < 64, totals[0], totals[1])

    def at_place(z):
        return (z * PLANE + place, sec)

    @pl.when(is_low)
    def _():
        pl.semaphore_wait(barrier, PLANE - 1 + SECTIONS - 1 + plane)

        def greet_later(z, carry):
            pl.semaphore_signal(barrier, inc=1, device_id=at_place(z), device_id_type=MESH)
            return carry

        def greet_earlier(z, carry):
            pl.semaphore_signal(
                ready_sem.at[plane], inc=1, device_id=at_place(z), device_id_type=MESH
            )
            return carry

        lax.fori_loop(plane + 1, PLANES, greet_later, 0)
        lax.fori_loop(0, plane, greet_earlier, 0)

    @pl.when(jnp.logical_not(is_low))
    def _():
        pl.semaphore_wait(barrier, SECTIONS - 1 + HALF)

    def power_copy(j):
        return pltpu.make_async_remote_copy(
            src_ref=pow_ref.at[SECTIONS],
            dst_ref=pow_ref.at[sec],
            send_sem=send_sem.at[0],
            recv_sem=recv_sem.at[0],
            device_id=(me, lax.rem(sec + j, SECTIONS)),
            device_id_type=MESH,
        )

    for j in range(1, SECTIONS):
        power_copy(j).start()
    for j in range(4):
        send_ref[j] = o_ref[j].astype(jnp.bfloat16).reshape(128, 2, 128)

    def block_copy(to, tiles):
        return pltpu.make_async_remote_copy(
            src_ref=send_ref.at[tiles, to],
            dst_ref=recv_ref.at[tiles, me],
            send_sem=send_sem.at[1],
            recv_sem=recv_sem.at[1],
            device_id=(to, sec),
            device_id_type=MESH,
        )

    body, tail, whole = pl.ds(0, 4), pl.ds(4, 1), pl.ds(0, 5)

    def send_plane(z, tiles, mates=False):
        for i in PLACES[: PLANE - 1] if mates else PLACES:
            block_copy(z * PLANE + lax.rem(place + i, PLANE), tiles).start()

    def send_low_half(tiles, first):
        def one(n, carry):
            send_plane(lax.rem(first + n, HALF), tiles)
            return carry

        lax.fori_loop(0, HALF, one, 0)

    @pl.when(jnp.logical_not(is_low))
    def _():
        mirror = PLANES - 1 - plane
        for i in PLACES:
            other = mirror * PLANE + lax.rem(place + i, PLANE)
            pl.semaphore_signal(high_sem, inc=1, device_id=(other, sec), device_id_type=MESH)
        send_low_half(body, plane)

    def bytes_of(ref, slot):
        return pltpu.make_async_remote_copy(
            src_ref=ref,
            dst_ref=ref,
            send_sem=send_sem.at[slot],
            recv_sem=recv_sem.at[slot],
            device_id=(me, sec),
            device_id_type=MESH,
        )

    three = bytes_of(pow_ref.at[pl.ds(0, SECTIONS - 1)], 0)
    three.wait_send()
    three.wait_recv()
    mine = lax.broadcasted_iota(jnp.int32, (1, 128), 1) * 0 + sec
    total = pow_ref[SECTIONS]
    for other in range(SECTIONS):
        total = total + jnp.where(mine == other, 0.0, pow_ref[other])
    mean = total * (1.0 / (SECTIONS * FRAMES * NCH))
    gain = jnp.where(flag_ref[0] == 1, 0.0, 1.0 / jnp.sqrt(mean + 1e-05))
    g0 = gain.astype(jnp.bfloat16).astype(jnp.float32)
    g1 = (gain - g0).astype(jnp.bfloat16).astype(jnp.float32)
    g2 = gain - g0 - g1
    row = lax.broadcasted_iota(jnp.int32, (8, 128), 0)
    col = lax.broadcasted_iota(jnp.int32, (8, 128), 1)
    patch = jnp.zeros((8, 128), jnp.float32)
    for at, g in ((0, g0), (1, g1), (2, g2)):
        pair = jnp.where(row % 2 == 0, g[:, 0:1], g[:, 64:65])
        patch = jnp.where(col == GAIN_LANE + at, pair, patch)
    patch = jnp.broadcast_to(patch[None], (INPUTS // 8, 8, 128)).reshape(INPUTS, 128)
    wide = lax.broadcasted_iota(jnp.int32, (INPUTS, 128), 1)
    tile = jnp.where(wide < GAIN_LANE, o_ref[4], patch)
    send_ref[4] = tile.astype(jnp.bfloat16).reshape(128, 2, 128)
    def send_ready(z):
        pl.semaphore_wait(ready_sem.at[z], 1)
        send_plane(z, whole)

    @pl.when(is_low)
    def _():
        def earlier(z, carry):
            send_plane(z, whole)
            return carry

        def later(z, carry):
            send_ready(z)
            return carry

        send_plane(plane, whole, mates=True)
        lax.fori_loop(0, plane, earlier, 0)
        lax.fori_loop(plane + 1, HALF, later, 0)

    @pl.when(jnp.logical_not(is_low))
    def _():
        send_low_half(tail, 0)

    own = pltpu.make_async_copy(send_ref.at[:, me], recv_ref.at[:, me], own_sem)
    own.start()
    for load in loads[8:]:
        load.wait()
    section_ref[...] = jnp.full((8, 128), choice_ref[sec]).astype(jnp.float32)
    make_weights(delays_ref[...], sec * NCH + me * PER_GROUP, w_ref)

    @pl.when(is_low)
    def _():
        mirror = PLANES - 1 - plane
        pl.semaphore_wait(high_sem, PLANE)
        for i in range(1, HALF):
            other = lax.rem(plane + i, HALF)
            pl.semaphore_signal(
                ready_sem.at[mirror], inc=1, device_id=at_place(other), device_id_type=MESH
            )
        send_plane(mirror, whole)

        def other_high(n, carry):
            send_ready(HALF + lax.rem(mirror + n, HALF))
            return carry

        lax.fori_loop(1, HALF - 1, other_high, 0)
        last = HALF + lax.rem(mirror + HALF - 1, HALF)
        pl.semaphore_wait(ready_sem.at[last], 1)
        pl.semaphore_signal(all_sem, inc=1, device_id=at_place(mirror), device_id_type=MESH)
        send_plane(last, whole)

    @pl.when(jnp.logical_not(is_low))
    def _():
        pl.semaphore_wait(all_sem, 1)
        send_plane(plane, whole, mates=True)

        def mates(n, carry):
            send_plane(HALF + lax.rem(plane + n, HALF), whole)
            return carry

        lax.fori_loop(1, HALF, mates, 0)

    own.wait()
    sent = bytes_of(send_ref.at[:, pl.ds(0, STATIONS - 1)], 1)
    sent.wait_send()
    landed = bytes_of(recv_ref.at[:, pl.ds(0, STATIONS - 1)], 1)
    landed.wait_recv()


def channelize(volts, band, delays, flags, section):
    outer_h, outer_l = split_const(outer_table())
    inner_h, inner_l = split_const(inner_table())
    inputs = [
        volts,
        band,
        delays,
        jnp.asarray(taper_table()),
        jnp.asarray(np.concatenate([outer_h, outer_l], axis=0)),
        jnp.asarray(twist_tables()),
        jnp.asarray(np.concatenate([inner_h, inner_l], axis=0)),
        jnp.asarray(spread_table(), jnp.bfloat16),
    ]
    swap = jnp.asarray(swap_table(), jnp.bfloat16)
    split = jnp.asarray(split_table(), jnp.bfloat16)
    operands = [
        pltpu.with_memory_space_constraint(x, pltpu.HBM)
        for x in inputs + [section, swap, split]
    ]
    vmem = pl.BlockSpec(memory_space=pltpu.VMEM)
    return pl.pallas_call(
        channelize_kernel,
        out_shape=(
            pltpu.VMEM((5, STATIONS, POLS, 128), jnp.bfloat16),
            pltpu.VMEM((PER_GROUP, INPUTS, BEAMS), jnp.bfloat16),
            pltpu.VMEM((8, 128), jnp.float32),
            pltpu.VMEM(swap.shape, swap.dtype),
            pltpu.VMEM(split.shape, split.dtype),
        ),
        in_specs=[pl.BlockSpec(memory_space=pltpu.SMEM)]
        + [pl.BlockSpec(memory_space=pltpu.HBM)] * len(operands),
        out_specs=(vmem,) * 5,
        scratch_shapes=[pltpu.VMEM(x.shape, x.dtype) for x in inputs]
        + [
            pltpu.SMEM(section.shape, section.dtype),
            pltpu.VMEM((384, 768), jnp.bfloat16),
            pltpu.VMEM((4, 576, 128), jnp.float32),
            pltpu.VMEM((5, 256, 128), jnp.float32),
            pltpu.VMEM((5, STATIONS, POLS, 128), jnp.bfloat16),
            pltpu.VMEM((5, 1, 128), jnp.float32),
            pltpu.SemaphoreType.DMA((len(operands) + 1,)),
            pltpu.SemaphoreType.DMA((2,)),
            pltpu.SemaphoreType.DMA((2,)),
            pltpu.SemaphoreType.DMA,
            pltpu.SemaphoreType.REGULAR((PLANES,)),
            pltpu.SemaphoreType.REGULAR,
            pltpu.SemaphoreType.REGULAR,
        ],
        compiler_params=pltpu.CompilerParams(
            collective_id=0, has_side_effects=True, vmem_limit_bytes=24 << 20
        ),
        name="channelize",
    )(flags, *operands)


def per_device(voltages, bandpass, station_flags, delays, section):
    volts = voltages.reshape(2, POLS, 624, 128).transpose(0, 2, 1, 3).reshape(2, 1248, 128)
    turned, weights, choice, swap, split = channelize(
        volts, bandpass, delays, station_flags, section
    )
    vis, tied = finish(choice, weights, turned.reshape(5, INPUTS, 128), swap, split)
    return (vis[None], tied[None])


def solution(mesh):
    return jax.shard_map(
        per_device,
        mesh=mesh,
        in_specs=(P(None, "stn", "sec", None, None), P("sec", None), P("stn"), P(), P()),
        out_specs=(P("sec", "stn", None, None), P("sec", "stn", None, None, None, None)),
        check_vma=False,
    )
```
